256 devices in a mesh: dp: 32 (over z_lo, y, x), tensor: 8 (over z_hi, core).
Axes of the slice: x: 4, y: 4, z: 8 (z_hi: 4, z_lo: 2; z = z_hi * 2 + z_lo), core: 2. Of those that a mesh axis runs over, the one named last changes fastest.
Arguments:
- rollout_rows: bfloat16 [16384, 4608], P(('dp', 'tensor')), may hold values from -6 to 6
- pack_dest: int32 [16384], P(('dp', 'tensor')), may hold values from 0 to 16383, as said below
- lengths: int32 [17], replicated, may hold values from 128 to 1536, as said below
- pattern: int32 [128, 128], P('dp'), may hold values from 0 to 1, as said below
- norm_gain: float32 [4608], replicated, may hold values from 0.1 to 1.9
- w_query: bfloat16 [4608, 2048], P(None, 'tensor'), may hold values from -0.1875 to 0.1875
- w_key: bfloat16 [4608, 1024], P(None, 'tensor'), may hold values from -0.1875 to 0.1875
- w_value: bfloat16 [4608, 1024], P(None, 'tensor'), may hold values from -0.09375 to 0.09375
- w_out: bfloat16 [2048, 4608], P('tensor'), may hold values from -0.125 to 0.125
- post_gain: float32 [4608], replicated, may hold values from 0.1 to 1.9
Outputs:
- layer_out: bfloat16 [16384, 4608], P(('dp', 'tensor'))
The draws below stay inside these ranges and needn't reach their ends.
Inputs may be any that keep to these rules, and one draw needn't show every extreme that they name: `pack_dest`: a permutation of the pack rows; a rollout row goes to a pack row of the same tensor index, and the 64 rollout rows of one device go to each dp index exactly 2 at a time. `lengths`: all multiples of 128, summing to 16384; the prompt is shorter than 512. pattern[q, q] = 1; pattern[q, k] = 1 only where k <= q and key block k lies in the first 512 pack rows or in a dp shard at most 3 before query block q's shard.
All inputs are finite; a program needn't handle non-finite values.
Results may differ from the reference program's by a relative error of at most 0.017.
Values may be sent and summed in bfloat16 or wider, within the bound.
No kernel may reach another device: no remote copies, remote signals or barrier semaphores. Data moves between devices by JAX's collectives and lax.ppermute only.
A program may use at most 128 MiB of HBM per device.

```python
import jax
import jax.numpy as jnp
from jax import lax

D = 4608
HD = 128
HEADS_Q = 16
HEADS_KV = 8
BLK = 128
RESP = 16
SEQ_DEV = 512
TOK_DEV = 64
PACK = 16384
NB = 128
N_DP = 32
N_TENSOR = 8


def tree_blocks(key):
    streams = jax.random.split(jax.random.fold_in(key, 17), 4)
    per_shard = SEQ_DEV // BLK
    block_total = SEQ_DEV * N_DP // BLK
    longest = 3 * per_shard
    others = RESP - 1
    prompt = jax.random.randint(streams[0], (1,), 1, per_shard).astype(jnp.int32)
    remaining = block_total - longest - prompt[0]
    base_len = remaining // others
    surplus = remaining % others
    ranking = jax.random.permutation(streams[1], others)
    resp_blocks = base_len + (ranking < surplus).astype(jnp.int32)
    largest_move = jnp.minimum(base_len - 1, longest - base_len - 2)
    moves = jax.random.randint(streams[2], (others // 2,), 0, 1 << 20) % (largest_move + 1)
    partner = jax.random.permutation(streams[3], others)
    change = jnp.zeros((others,), jnp.int32)
    change = change.at[partner[:others // 2]].add(moves)
    change = change.at[partner[others // 2:2 * (others // 2)]].add(-moves)
    resp_blocks = (resp_blocks + change).astype(jnp.int32)
    return jnp.concatenate([prompt, jnp.array([longest], jnp.int32), resp_blocks]).astype(jnp.int32)


def draw_lengths(key, part):
    return (tree_blocks(key) * BLK).astype(jnp.int32)


def draw_pattern(key, part):
    resp_blocks = tree_blocks(key)
    block_total = SEQ_DEV * N_DP // BLK
    bounds = jnp.cumsum(resp_blocks).astype(jnp.int32)
    block_ids = jnp.arange(block_total, dtype=jnp.int32)
    segment = jnp.sum((block_ids[:, None] >= bounds[None, :]).astype(jnp.int32), axis=1)
    visible = (block_ids[None, :] <= block_ids[:, None]) & ((segment[None, :] == 0) | (segment[None, :] == segment[:, None]))
    return visible.astype(jnp.int32)


def shuffled(streams_key, count):

    def single(one_key):
        return jax.random.permutation(one_key, TOK_DEV)
    return jax.vmap(single)(jax.random.split(streams_key, count))


def draw_pack_dest(key, part):
    streams = jax.random.split(jax.random.fold_in(key, 29), 3)
    per_peer = TOK_DEV // N_DP
    count = N_DP * N_TENSOR
    slot_perm = shuffled(streams[0], count).reshape(N_DP, N_TENSOR, TOK_DEV)
    source_dev = jnp.arange(N_DP, dtype=jnp.int32)[:, None, None]
    tensor_ids = jnp.arange(N_TENSOR, dtype=jnp.int32)[None, :, None]
    column = slot_perm // per_peer
    within = slot_perm % per_peer
    dev_perm = jax.random.permutation(streams[1], N_DP)
    target = dev_perm[(source_dev + column) % N_DP]
    arrival = source_dev * per_peer + within
    land_perm = shuffled(streams[2], count).reshape(N_DP, N_TENSOR, TOK_DEV)
    tensor_full = jnp.broadcast_to(tensor_ids, target.shape)
    landing = land_perm[target, tensor_full, arrival]
    dest = (target * N_TENSOR + tensor_full) * TOK_DEV + landing
    return dest.reshape(-1).astype(jnp.int32)


def shard_levels(own_key, dims, cuts, smallest, top_value):
    level = 1.0
    for dim, shards_of in cuts:
        heights = jax.random.uniform(jax.random.fold_in(jax.random.fold_in(own_key, 6), dim), (shards_of,), jnp.float32, smallest / len(cuts), top_value / len(cuts))
        level = level * jnp.repeat(jnp.exp(heights), dims[dim] // shards_of).reshape((-1,) + (1,) * (len(dims) - 1 - dim))
    return level


def gaussian(key, shape, width, reach, shards=(), held_as=jnp.bfloat16):
    drawn = jax.random.normal(key, shape, jnp.float32) * width
    if len(shards) > 0:
        drawn = shard_levels(key, shape, shards, -0.22, 0.18) * drawn
    return jnp.clip(drawn, min=-reach, max=reach).astype(held_as)


def setup_inputs(seed: int = 0) -> dict:
    key_list = jax.random.split(jax.random.key(seed), 11)
    rollout_rows = gaussian(key_list[0], (PACK, D), 1.0, 6.0, ((0, 256),))
    pack_dest = draw_pack_dest(jax.random.fold_in(key_list[10], 71), 0)
    lengths = draw_lengths(jax.random.fold_in(key_list[10], 71), 0)
    pattern = draw_pattern(jax.random.fold_in(key_list[10], 71), 0)
    norm_gain = jnp.clip(1.0 + 0.18 * jax.random.normal(key_list[4], (D,), jnp.float32), 0.1, 1.9)
    w_query = gaussian(key_list[5], (D, HEADS_Q * HD), (D // 5) ** -0.5, 0.1875, ((1, 8),))
    w_key = gaussian(key_list[6], (D, HEADS_KV * HD), (D // 5) ** -0.5, 0.1875, ((1, 8),))
    w_value = gaussian(key_list[7], (D, HEADS_KV * HD), D ** -0.5, 0.09375, ((1, 8),))
    w_out = gaussian(key_list[8], (HEADS_Q * HD, D), (HEADS_Q * HD) ** -0.5, 0.125, ((0, 8),))
    post_gain = jnp.clip(1.0 + 0.18 * jax.random.normal(key_list[9], (D,), jnp.float32), 0.1, 1.9)
    return {"rollout_rows": rollout_rows, "pack_dest": pack_dest, "lengths": lengths, "pattern": pattern, "norm_gain": norm_gain, "w_query": w_query, "w_key": w_key, "w_value": w_value, "w_out": w_out, "post_gain": post_gain}


SOFT_CAP = 50.0
QUERY_SCALE = 1.0 / 12.0
ROPE_BASE = 10000.0
EPSILON = 1e-06

def positions(row_ids, lengths):
    bounds = jnp.cumsum(lengths).astype(jnp.int32)
    prompt = lengths[0]
    passed = (row_ids[:, None] >= bounds[None, :]).astype(jnp.int32)
    offset_start = lax.optimization_barrier(jnp.sum(passed * lengths[None, :], axis=1)).astype(jnp.int32)
    return jnp.where(row_ids < prompt, row_ids, prompt + row_ids - offset_start)

def rotate(values, angle_pos):
    half_width = values.shape[-1] // 2
    inverse_freq = jnp.power(ROPE_BASE, -(jnp.arange(half_width, dtype=jnp.float32) * 2.0) / values.shape[-1])
    angles = angle_pos[:, None] * inverse_freq[None, :]
    cosine = jnp.cos(angles)[:, None, :]
    sine_part = jnp.sin(angles)[:, None, :]
    front_half = values[..., :half_width]
    back_half = values[..., half_width:]
    return jnp.concatenate([front_half * cosine - back_half * sine_part, back_half * cosine + front_half * sine_part], axis=-1)

def rms_scale(values, gain):
    return values * lax.rsqrt(lax.optimization_barrier(jnp.mean(values * values, axis=-1, keepdims=True)) + EPSILON) * gain

def attend(running, queries, key_value, pats, q_start, k_start, low_block, high_block):
    query_count = queries.shape[0]
    head_count = queries.shape[1]
    head_width = queries.shape[3]
    block_count = key_value.shape[0] // BLK
    key_blocks = key_value.reshape(block_count, BLK, 2, head_count, head_width)
    q_ids = q_start + jnp.arange(query_count, dtype=jnp.int32)
    first_block = k_start // BLK
    highest = lax.Precision.HIGHEST

    def step(block_index, current):
        block_id = first_block + block_index
        column = lax.dynamic_index_in_dim(pats, jnp.clip(block_id, 0, pats.shape[1] - 1), 1, keepdims=False)
        active = (block_id >= low_block) & (block_id < high_block) & jnp.any(column == 1)

        def compute(inner):
            weighted, totals = inner
            block_pair = lax.dynamic_index_in_dim(key_blocks, block_index, 0, keepdims=False)
            key_tile = block_pair[:, 0].astype(jnp.float32)
            value_tile = block_pair[:, 1].astype(jnp.float32)
            scores = jnp.einsum('qhgd,khd->hgqk', queries, key_tile, precision=highest) * QUERY_SCALE
            capped = SOFT_CAP * jnp.tanh(scores / SOFT_CAP)
            k_ids = block_id * BLK + jnp.arange(BLK, dtype=jnp.int32)
            allowed = (jnp.repeat(column, BLK) == 1)[:, None] & (k_ids[None, :] <= q_ids[:, None])
            weights = jnp.where(allowed, jnp.exp(capped), jnp.float32(0.0))
            rounded = lax.optimization_barrier(weights.astype(jnp.bfloat16)).astype(jnp.float32)
            weighted = weighted + jnp.einsum('hgqk,khd->hgqd', rounded, value_tile, precision=highest)
            totals = totals + lax.optimization_barrier(jnp.sum(weights, axis=-1))
            return (weighted, totals)
        return lax.cond(active, compute, lambda inner: inner, current)
    return lax.fori_loop(0, block_count, step, running)

def reference(rollout_rows, pack_dest, lengths, pattern, norm_gain, w_query, w_key, w_value, w_out, post_gain):
    highest = lax.Precision.HIGHEST
    packed = jnp.zeros_like(rollout_rows).at[pack_dest].set(rollout_rows)
    normed = rms_scale(packed.astype(jnp.float32), norm_gain).astype(jnp.bfloat16)
    normed = lax.optimization_barrier(normed).astype(jnp.float32)
    row_ids = jnp.arange(PACK, dtype=jnp.int32)
    angle_pos = positions(row_ids, lengths).astype(jnp.float32)
    query_all = jnp.dot(normed, w_query.astype(jnp.float32), precision=highest)
    query_all = rotate(query_all.reshape(PACK, HEADS_Q, HD), angle_pos).astype(jnp.bfloat16)
    key_all = jnp.dot(normed, w_key.astype(jnp.float32), precision=highest)
    key_all = rotate(key_all.reshape(PACK, HEADS_KV, HD), angle_pos).reshape(PACK, HEADS_KV * HD).astype(jnp.bfloat16)
    value_all = jnp.dot(normed, w_value.astype(jnp.float32), precision=highest).astype(jnp.bfloat16)
    key_value = jnp.concatenate([key_all, value_all], axis=1).reshape(N_DP, SEQ_DEV, 2 * HEADS_KV * HD)
    group_size = HEADS_Q // HEADS_KV
    query_shards = query_all.astype(jnp.float32).reshape(N_DP, SEQ_DEV, HEADS_KV, group_size, HD)
    pat_shards = pattern.reshape(N_DP, SEQ_DEV // BLK, NB)
    shard_ids = jnp.arange(N_DP, dtype=jnp.int32)

    def one_shard(inputs):
        shard_index, queries, pats = inputs
        start_state = (jnp.zeros((HEADS_KV, group_size, SEQ_DEV, HD), jnp.float32), jnp.zeros((HEADS_KV, group_size, SEQ_DEV), jnp.float32))

        def over(current, scan_item):
            source, block_pair = scan_item
            return (attend(current, queries, block_pair, pats, shard_index * SEQ_DEV, source * SEQ_DEV, 0, NB), None)
        (weighted, totals), _ = lax.scan(over, start_state, (shard_ids, key_value))
        attended = weighted / totals[..., None]
        return jnp.transpose(attended, (2, 0, 1, 3)).reshape(SEQ_DEV, HEADS_Q * HD).astype(jnp.bfloat16)
    heads_out = lax.map(one_shard, (shard_ids, query_shards, pat_shards)).reshape(PACK, HEADS_Q * HD)
    slice_width = HEADS_Q * HD // N_TENSOR
    summed = jnp.zeros((PACK, D), jnp.float32)
    for shard in range(N_TENSOR):
        out_term = jnp.dot(heads_out[:, shard * slice_width:(shard + 1) * slice_width].astype(jnp.float32), w_out[shard * slice_width:(shard + 1) * slice_width].astype(jnp.float32), precision=highest)
        summed = summed + lax.optimization_barrier(out_term.astype(jnp.bfloat16)).astype(jnp.float32)
    result = packed.astype(jnp.float32) + rms_scale(summed, post_gain)
    return result.astype(jnp.bfloat16)
```

```python
import functools
import math

import jax
import jax.numpy as jnp
from jax import lax
from jax.experimental import pallas as pl
from jax.experimental.pallas import tpu as pltpu
from jax.sharding import PartitionSpec as P

HD = 128
BLK = 128
D = 4608
SHARD = 512
SLOTS = 64
PLANES = 4
RING = 16

SOFT_CAP = 50.0
QUERY_SCALE = 1.0 / 12.0
ROPE_BASE = 10000.0
EPSILON = 1e-06

NEXT = [(t, (t + 2) % 8) for t in range(8)]
PREV = [(t, (t + 6) % 8) for t in range(8)]
FAR = [(t, (t + 4) % 8) for t in range(8)]
SIB = [(t, t ^ 1) for t in range(8)]
VMEM_BYTES = 56 << 20


def positions(row_ids, lengths):
    bounds = jnp.cumsum(lengths)
    prompt = lengths[0]
    passed = (row_ids[:, None] >= bounds[None, :]).astype(jnp.int32)
    offset_start = jnp.sum(passed * lengths[None, :], axis=1)
    return jnp.where(row_ids < prompt, row_ids, prompt + row_ids - offset_start)


def rope_tables(row_ids, lengths):
    angle_pos = positions(row_ids, lengths).astype(jnp.float32)
    half = HD // 2
    inverse_freq = jnp.power(ROPE_BASE, -(jnp.arange(half, dtype=jnp.float32) * 2.0) / HD)
    angles = angle_pos[:, None] * inverse_freq[None, :]
    cosine = jnp.cos(angles)
    sine = jnp.sin(angles)
    return jnp.concatenate([cosine, cosine], 1), jnp.concatenate([-sine, sine], 1)


def rms_scale(values, gain):
    return values * lax.rsqrt(jnp.mean(values * values, axis=-1, keepdims=True) + EPSILON) * gain


def to(values, pairs):
    return lax.ppermute(values, "tensor", pairs)


def qkv_kernel(count, *refs):
    xs = refs[:count]
    wq, wk, wv, cos, sin, q_out, kv_out, acc = refs[count:]
    step = pl.program_id(0)

    @pl.when(step == 0)
    def _():
        acc[...] = jnp.zeros_like(acc)

    x = jnp.concatenate([r[...] for r in xs], axis=0)
    acc[:, :256] += jnp.dot(x, wq[...], preferred_element_type=jnp.float32)
    acc[:, 256:384] += jnp.dot(x, wk[...], preferred_element_type=jnp.float32)
    acc[:, 384:] += jnp.dot(x, wv[...], preferred_element_type=jnp.float32)

    @pl.when(step == pl.num_programs(0) - 1)
    def _():
        c = cos[...]
        s = sin[...]

        def turn(v):
            return (v * c + pltpu.roll(v, HD // 2, 1) * s).astype(jnp.bfloat16)

        q_out[0] = turn(acc[:, :128])
        q_out[1] = turn(acc[:, 128:256])
        kv_out[:, :128] = turn(acc[:, 256:384])
        kv_out[:, 128:] = acc[:, 384:].astype(jnp.bfloat16)


def project(pieces, w_query, w_key, w_value, cos, sin):
    rows = sum(p.shape[0] for p in pieces)
    tile = 512
    in_specs = [pl.BlockSpec((p.shape[0], tile), lambda k: (0, k)) for p in pieces]
    in_specs += [pl.BlockSpec((tile, w.shape[1]), lambda k: (k, 0)) for w in (w_query, w_key, w_value)]
    in_specs += [pl.BlockSpec((rows, HD), lambda k: (0, 0))] * 2
    return pl.pallas_call(
        functools.partial(qkv_kernel, len(pieces)),
        grid=(D // tile,),
        in_specs=in_specs,
        out_specs=[
            pl.BlockSpec((2, rows, HD), lambda k: (0, 0, 0)),
            pl.BlockSpec((rows, 2 * HD), lambda k: (0, 0)),
        ],
        out_shape=[
            jax.ShapeDtypeStruct((2, rows, HD), jnp.bfloat16),
            jax.ShapeDtypeStruct((rows, 2 * HD), jnp.bfloat16),
        ],
        scratch_shapes=[pltpu.VMEM((rows, 512), jnp.float32)],
        compiler_params=pltpu.CompilerParams(vmem_limit_bytes=VMEM_BYTES),
        name="project",
    )(*pieces, w_query, w_key, w_value, cos, sin)


def attend_kernel(tab, core, q_a, q_c, *refs):
    kvs = refs[:8]
    prompt = refs[8]
    outs = refs[9:13]
    q2, acc, tot = refs[13:]
    for head in range(2):
        q2[head * 512 : head * 512 + 384] = q_a[head]
        q2[head * 512 + 384 : head * 512 + 512] = q_c[head]
    acc[...] = jnp.zeros_like(acc)
    tot[...] = jnp.zeros_like(tot)
    c = core[0]

    def block(ref, row, column, diagonal):
        flags = [tab[i, column] for i in range(PLANES)]

        @pl.when(flags[0] + flags[1] + flags[2] + flags[3] > 0)
        def _():
            k = ref[row : row + BLK, :HD]
            v = ref[row : row + BLK, HD:]
            scores = lax.dot_general(
                q2[...], k, (((1,), (1,)), ((), ())), preferred_element_type=jnp.float32
            )
            weights = jnp.exp2(jnp.tanh(scores * (QUERY_SCALE / SOFT_CAP)) * (SOFT_CAP * math.log2(math.e)))
            parts = []
            for i in range(2 * PLANES):
                part = weights[i * BLK : (i + 1) * BLK]
                if i % PLANES == diagonal:
                    rows_id = lax.broadcasted_iota(jnp.int32, (BLK, BLK), 0)
                    cols_id = lax.broadcasted_iota(jnp.int32, (BLK, BLK), 1)
                    flip = c * SLOTS
                    part = jnp.where((cols_id ^ flip) <= (rows_id ^ flip), part, 0.0)
                parts.append(part * flags[i % PLANES].astype(jnp.float32))
            weights = jnp.concatenate(parts, axis=0)
            tot[...] += weights
            acc[...] += jnp.dot(weights.astype(jnp.bfloat16), v, preferred_element_type=jnp.float32)

    for source in range(4):
        for b in range(PLANES):
            ref, row = (kvs[2 * source], b * BLK) if b < 3 else (kvs[2 * source + 1], 0)
            block(ref, row, source * PLANES + b, b if source == 0 else -1)
    for b in range(PLANES):
        block(prompt, b * BLK, 4 * PLANES + b, -1)
    for head in range(2):
        for i in range(PLANES):
            lo = head * 512 + i * BLK
            total = jnp.sum(tot[lo : lo + BLK], axis=1, keepdims=True)
            outs[i][:, head * HD : (head + 1) * HD] = (acc[lo : lo + BLK] / total).astype(jnp.bfloat16)


def attend(tab, core, q_a, q_c, kvs, prompt):
    smem = pl.BlockSpec(memory_space=pltpu.SMEM)
    vmem = pl.BlockSpec(memory_space=pltpu.VMEM)
    return pl.pallas_call(
        attend_kernel,
        in_specs=[smem, smem] + [vmem] * 11,
        out_specs=[vmem] * 4,
        out_shape=[jax.ShapeDtypeStruct((BLK, 2 * HD), jnp.bfloat16)] * 4,
        scratch_shapes=[
            pltpu.VMEM((1024, HD), jnp.bfloat16),
            pltpu.VMEM((1024, HD), jnp.float32),
            pltpu.VMEM((1024, HD), jnp.float32),
        ],
        compiler_params=pltpu.CompilerParams(vmem_limit_bytes=VMEM_BYTES),
        name="attend",
    )(tab, core, q_a, q_c, *kvs, prompt)


def out_kernel(a0, a1, a2, a3, w0, wg, mine, other):
    total = jnp.dot(a0[...], w0[...], preferred_element_type=jnp.float32)
    for i, a in enumerate((a1, a2, a3)):
        w = wg[:, i].reshape(2 * HD, w0.shape[1])
        total += jnp.dot(a[...], w, preferred_element_type=jnp.float32)
    mine[...] = total[:SLOTS]
    other[...] = total[SLOTS:].astype(jnp.bfloat16)


def project_out(parts, w_own, w_far):
    tile = 512
    return pl.pallas_call(
        out_kernel,
        grid=(D // tile,),
        in_specs=[pl.BlockSpec((BLK, 2 * HD), lambda n: (0, 0))] * 4
        + [
            pl.BlockSpec((2 * HD, tile), lambda n: (0, n)),
            pl.BlockSpec((RING, 3, 2 * HD // RING, tile), lambda n: (0, 0, 0, n)),
        ],
        out_specs=[pl.BlockSpec((SLOTS, tile), lambda n: (0, n))] * 2,
        out_shape=[
            jax.ShapeDtypeStruct((SLOTS, D), jnp.float32),
            jax.ShapeDtypeStruct((SLOTS, D), jnp.bfloat16),
        ],
        compiler_params=pltpu.CompilerParams(vmem_limit_bytes=VMEM_BYTES),
        name="project_out",
    )(*parts, w_own, w_far)


def body(
    rollout_rows, pack_dest, lengths, pattern, norm_gain, w_query, w_key, w_value, w_out, post_gain
):
    bf16 = jnp.bfloat16
    n_dp = lax.axis_size("dp")
    d = lax.axis_index("dp")
    t = lax.axis_index("tensor")
    plane = t // 2
    core = t % 2
    per_peer = SLOTS // n_dp
    order_ids = jnp.arange(SLOTS, dtype=jnp.int32)

    target_dev = pack_dest // SHARD
    target_slot = pack_dest % SLOTS
    before = (target_dev[:, None] == target_dev[None, :]) & (order_ids[None, :] < order_ids[:, None])
    send_pos = target_dev * per_peer + jnp.sum(before.astype(jnp.int32), axis=1)
    placer = order_ids[:, None] == send_pos[None, :]
    send_rows = jnp.dot(placer.astype(bf16), rollout_rows, preferred_element_type=jnp.float32).astype(bf16)
    send_slots = jnp.sum(jnp.where(placer, target_slot[None, :], 0), axis=1)
    send = jnp.concatenate(
        [send_rows, jnp.broadcast_to(send_slots.astype(bf16)[:, None], (SLOTS, HD))], axis=1
    )
    width = D + HD
    got = lax.all_to_all(send.reshape(n_dp, per_peer, width), "dp", 0, 0, tiled=True).reshape(SLOTS, width)

    xy = d % RING
    rows_each = w_out.shape[0] // RING
    piece = lax.dynamic_slice_in_dim(w_out, xy * rows_each, rows_each, 0)
    far = jnp.concatenate([to(piece, NEXT), to(piece, PREV), to(piece, FAR)], axis=0)
    groups = [list(range(g * RING, (g + 1) * RING)) for g in range(n_dp // RING)]
    w_far = lax.all_gather(far, "dp", axis=0, tiled=True, axis_index_groups=groups)
    w_far = w_far.reshape(RING, 3, rows_each, D)

    early = lax.all_to_all(
        jnp.broadcast_to(send[None, :per_peer], (8, per_peer, width)), "tensor", 0, 0, tiled=True
    )
    early_rows = early[..., :D].reshape(8 * per_peer, D)
    early_slot = early[..., D].astype(jnp.int32)
    early_pos = (jnp.arange(8, dtype=jnp.int32)[:, None] * SLOTS + early_slot).reshape(-1)
    early_norm = rms_scale(early_rows.astype(jnp.float32), norm_gain).astype(bf16)
    ecos, esin = rope_tables(early_pos, lengths)
    early_k = jnp.dot(early_norm, w_key, preferred_element_type=jnp.float32)
    early_k = early_k * ecos + jnp.roll(early_k, HD // 2, axis=1) * esin
    early_v = jnp.dot(early_norm, w_value, preferred_element_type=jnp.float32)
    early_kv = jnp.concatenate([early_k, early_v], axis=1).astype(bf16)
    prompt = lax.all_to_all(
        jnp.broadcast_to(early_kv[None], (n_dp,) + early_kv.shape), "dp", 0, 0, tiled=True
    )
    prompt = prompt.reshape(n_dp, 8, per_peer, 2 * HD).transpose(1, 0, 2, 3).reshape(SHARD, 2 * HD)

    order = jnp.stack([plane, plane + 3, plane + 1, plane + 2]) % PLANES
    local = jnp.arange(SHARD, dtype=jnp.int32)
    row_ids = (
        d * SHARD
        + order[local // BLK] * BLK
        + ((local % BLK) ^ (core * SLOTS))
    )
    cos, sin = rope_tables(row_ids, lengths)

    arrange = order_ids[:, None] == got[:, D].astype(jnp.int32)[None, :]
    packed = jnp.dot(arrange.astype(bf16), got[:, :D], preferred_element_type=jnp.float32).astype(bf16)
    normed = rms_scale(packed.astype(jnp.float32), norm_gain).astype(bf16)

    half = SLOTS // 2
    near_p = to(normed, NEXT)
    near_n = to(normed, PREV)
    own_s = to(normed, SIB)
    near_ps = to(near_p, SIB)
    near_ns = to(near_n, SIB)
    q_a, kv_a = project(
        [normed, own_s, near_p, near_ps, near_n, near_ns], w_query, w_key, w_value, cos[:384], sin[:384]
    )
    far_top = to(near_p[:half], NEXT)
    far_bot = to(near_n[half:], PREV)
    far_own = jnp.concatenate([far_top, far_bot], axis=0)
    far_s = to(far_own, SIB)
    q_c, kv_c = project([far_own, far_s], w_query, w_key, w_value, cos[384:], sin[384:])

    kvs = [kv_a, kv_c]
    for k in (1, 2, 3):
        shift = [(s, s + k) for s in range(n_dp - k)]
        kvs += [lax.ppermute(kv_a, "dp", shift), lax.ppermute(kv_c, "dp", shift)]

    pat = pattern[order]
    columns = []
    valid = []
    for k in range(4):
        columns.append(jnp.maximum(d - k, 0) * PLANES + order)
        valid.append(jnp.broadcast_to((d - k >= 1) | (k == 0), (PLANES,)))
    columns.append(jnp.arange(PLANES, dtype=jnp.int32))
    valid.append(jnp.broadcast_to(d >= 1, (PLANES,)))
    tab = (pat[:, jnp.concatenate(columns)] == 1) & jnp.concatenate(valid)[None, :]
    parts = attend(tab.astype(jnp.int32), core.reshape(1).astype(jnp.int32), q_a, q_c, kvs, prompt)

    mine, other = project_out(
        [parts[0], to(parts[2], NEXT), to(parts[1], PREV), to(parts[3], FAR)], w_out, w_far
    )
    summed = mine + to(other, SIB).astype(jnp.float32)
    result = packed.astype(jnp.float32) + rms_scale(summed, post_gain)
    return result.astype(bf16)


def solution(mesh):
    placed = (
        P(("dp", "tensor"), None),
        P(("dp", "tensor")),
        P(),
        P("dp", None),
        P(),
        P(None, "tensor"),
        P(None, "tensor"),
        P(None, "tensor"),
        P("tensor", None),
        P(),
    )
    return jax.shard_map(
        body, mesh=mesh, in_specs=placed, out_specs=P(("dp", "tensor"), None), check_vma=False
    )
```

```python
import functools
import math

import jax
import jax.numpy as jnp
import numpy as np
from jax import lax
from jax.experimental import pallas as pl
from jax.experimental.pallas import tpu as pltpu
from jax.sharding import PartitionSpec as P

HD = 128
BLK = 128
D = 4608
SHARD = 512
SLOTS = 64
PLANES = 4

SOFT_CAP = 50.0
QUERY_SCALE = 1.0 / 12.0
ROPE_BASE = 10000.0
EPSILON = 1e-06

OUT = [(t, (t + (6 if t % 2 else 2)) % 8) for t in range(8)]
BACK = [(t, (t + (2 if t % 2 else 6)) % 8) for t in range(8)]
FAR = [(t, (t + 4) % 8) for t in range(8)]
SIB = [(t, t ^ 1) for t in range(8)]
VMEM_BYTES = 16 << 20
TILES = 6
OTHER = (0, 2, 1, 3)


SMEM = pl.BlockSpec(memory_space=pltpu.SMEM)
VMEM = pl.BlockSpec(memory_space=pltpu.VMEM)


def inverse_freq():
    half = HD // 2
    steps = np.arange(half, dtype=np.float32) * np.float32(2.0) / np.float32(HD)
    freq = np.power(np.float32(ROPE_BASE), -steps).astype(np.float32)
    return jnp.asarray(np.concatenate([freq, freq])[None, :])


def rope(row_ids, lengths, freq):
    bound = lengths[0]
    past = jnp.where(row_ids >= bound, lengths[0], 0)
    for i in range(1, lengths.shape[0]):
        bound = bound + lengths[i]
        past = past + jnp.where(row_ids >= bound, lengths[i], 0)
    place = jnp.where(row_ids < lengths[0], row_ids, lengths[0] + row_ids - past)
    angles = place.astype(jnp.float32) * freq
    lane = lax.broadcasted_iota(jnp.int32, row_ids.shape, 1)
    sine = jnp.sin(angles)
    return jnp.cos(angles), jnp.where(lane < HD // 2, -sine, sine)


def plane_order():
    t = lax.axis_index("tensor")
    plane = t // 2
    core = t % 2
    side = 1 - 2 * core
    return core, [plane] + [(plane + PLANES + k) % PLANES for k in (-side, side, 2)]


def tables_kernel(lengths, freq, cos_a, sin_a, cos_c, sin_c):
    core, order = plane_order()
    base = lax.axis_index("dp") * SHARD
    local = lax.broadcasted_iota(jnp.int32, (BLK, HD), 0) ^ (core * SLOTS)
    for i in range(PLANES):
        c, s = rope(base + order[i] * BLK + local, lengths, freq[...])
        if i < 3:
            cos_a[i * BLK : (i + 1) * BLK] = c
            sin_a[i * BLK : (i + 1) * BLK] = s
        else:
            cos_c[...] = c
            sin_c[...] = s


def tables(lengths):
    return pl.pallas_call(
        tables_kernel,
        in_specs=[SMEM, VMEM],
        out_specs=[VMEM] * 4,
        out_shape=[jax.ShapeDtypeStruct((n, HD), jnp.float32) for n in (384, 384, BLK, BLK)],
        compiler_params=pltpu.CompilerParams(vmem_limit_bytes=VMEM_BYTES),
        name="tables",
    )(lengths, inverse_freq())


def early_kernel(lengths, freq, own, sib, gain, wk, wv, out):
    core, order = plane_order()
    rows = jnp.concatenate([own[...], sib[...]], axis=0)
    x = rms_scale(rows[:, :D].astype(jnp.float32), gain[...]).astype(jnp.bfloat16)
    slot = rows[:, D:].astype(jnp.int32)
    index = lax.broadcasted_iota(jnp.int32, slot.shape, 0) // 2
    source = jnp.zeros_like(index)
    for i in range(2 * PLANES):
        source = jnp.where(index == i, early_source(i, core, order), source)
    c, s = rope(source * SLOTS + slot, lengths, freq[...])
    kv = jnp.dot(x, jnp.concatenate([wk[...], wv[...]], axis=1), preferred_element_type=jnp.float32)
    k = kv[:, :HD]
    k = k * c + pltpu.roll(k, HD // 2, 1) * s
    both = jnp.concatenate([k, kv[:, HD:]], axis=1).astype(jnp.bfloat16)
    out[...] = jnp.broadcast_to(both[None], out.shape)


def early_source(i, core, order):
    if i < PLANES:
        return 2 * order[i] + core
    return 2 * order[OTHER[i - PLANES]] + 1 - core


def early_keys(lengths, own, sib, gain, w_key, w_value, copies):
    return pl.pallas_call(
        early_kernel,
        in_specs=[SMEM] + [VMEM] * 6,
        out_specs=VMEM,
        out_shape=jax.ShapeDtypeStruct((copies, 2 * own.shape[0], 2 * HD), jnp.bfloat16),
        compiler_params=pltpu.CompilerParams(vmem_limit_bytes=VMEM_BYTES),
        name="early",
    )(lengths, inverse_freq(), own, sib, gain[None, :], w_key, w_value)


def rms_scale(values, gain):
    return values * lax.rsqrt(jnp.mean(values * values, axis=-1, keepdims=True) + EPSILON) * gain


def to(values, pairs):
    return lax.ppermute(values, "tensor", pairs)


def qkv(pieces, wq, wk, wv, cos, sin):
    x = jnp.concatenate([r[...] for r in pieces], axis=0)
    c = cos[...]
    s = sin[...]

    def turn(v):
        return (v * c + pltpu.roll(v, HD // 2, 1) * s).astype(jnp.bfloat16)

    q = jnp.dot(x, wq[...], preferred_element_type=jnp.float32)
    wkv = jnp.concatenate([wk[...], wv[...]], axis=1)
    kv = jnp.dot(x, wkv, preferred_element_type=jnp.float32)
    return turn(q[:, :HD]), turn(q[:, HD:]), turn(kv[:, :HD]), kv[:, HD:].astype(jnp.bfloat16)


def near_kernel(x0, x1, x2, x3, x4, x5, wq, wk, wv, cos, sin, q_out, kv_out):
    q0, q1, k, v = qkv((x0, x1, x2, x3, x4, x5), wq, wk, wv, cos, sin)
    q_out[0] = q0
    q_out[1] = q1
    kv_out[:, :HD] = k
    kv_out[:, HD:] = v


def far_kernel(x0, x1, wq, wk, wv, cos, sin, q_in, kv_in, q_out, kv_out):
    q0, q1, k, v = qkv((x0, x1), wq, wk, wv, cos, sin)
    near = SHARD - BLK
    q_out[:near] = q_in[0]
    q_out[near:SHARD] = q0
    q_out[SHARD : SHARD + near] = q_in[1]
    q_out[SHARD + near :] = q1
    kv_out[:near] = kv_in[...]
    kv_out[near:, :HD] = k
    kv_out[near:, HD:] = v


def project_near(*args):
    rows = SHARD - BLK
    return pl.pallas_call(
        near_kernel,
        in_specs=[VMEM] * len(args),
        out_specs=[VMEM] * 2,
        out_shape=[
            jax.ShapeDtypeStruct((2, rows, HD), jnp.bfloat16),
            jax.ShapeDtypeStruct((rows, 2 * HD), jnp.bfloat16),
        ],
        compiler_params=pltpu.CompilerParams(vmem_limit_bytes=VMEM_BYTES),
        name="project_near",
    )(*args)


def project_far(*args):
    return pl.pallas_call(
        far_kernel,
        in_specs=[VMEM] * len(args),
        out_specs=[VMEM] * 2,
        out_shape=[
            jax.ShapeDtypeStruct((2 * SHARD, HD), jnp.bfloat16),
            jax.ShapeDtypeStruct((SHARD, 2 * HD), jnp.bfloat16),
        ],
        compiler_params=pltpu.CompilerParams(vmem_limit_bytes=VMEM_BYTES),
        name="project_far",
    )(*args)


def attend_kernel(pattern, q2, *refs):
    kvs = refs[:4]
    prompt = refs[4]
    ours, theirs, acc, tot = refs[5:]
    acc[...] = jnp.zeros_like(acc)
    tot[...] = jnp.zeros_like(tot)
    core, order = plane_order()
    d = lax.axis_index("dp")
    lane = lax.broadcasted_iota(jnp.int32, (1, BLK), 1)

    def block(ref, row, some, masks):
        @pl.when(some)
        def _():
            k = ref[row : row + BLK, :HD]
            v = ref[row : row + BLK, HD:]
            scores = lax.dot_general(
                q2[...], k, (((1,), (1,)), ((), ())), preferred_element_type=jnp.float32
            )
            weights = jnp.exp2(jnp.tanh(scores * (QUERY_SCALE / SOFT_CAP)) * (SOFT_CAP * math.log2(math.e)))
            parts = []
            for i in range(2 * PLANES):
                parts.append(masks[i % PLANES](weights[i * BLK : (i + 1) * BLK]))
            weights = jnp.concatenate(parts, axis=0)
            tot[...] += weights
            acc[...] += jnp.dot(weights.astype(jnp.bfloat16), v, preferred_element_type=jnp.float32)

    def scaled(flag):
        return lambda part: part * flag.astype(jnp.float32)

    def causal(flag):
        def mask(part):
            flip = core * SLOTS
            rows_id = lax.broadcasted_iota(jnp.int32, (BLK, BLK), 0) ^ flip
            cols_id = lax.broadcasted_iota(jnp.int32, (BLK, BLK), 1) ^ flip
            return jnp.where(cols_id <= rows_id, part, 0.0) * flag.astype(jnp.float32)

        return mask

    def seen(i, shard, plane):
        return (pattern[order[i], shard * PLANES + plane] == 1).astype(jnp.int32)

    for source in range(4):
        shard = jnp.maximum(d - source, 0)
        for b in range(PLANES):
            flags = [seen(i, shard, order[b]) for i in range(PLANES)]
            some = flags[0] + flags[1] + flags[2] + flags[3] > 0
            if source:
                some = some & (d - source >= 1)
            masks = [causal(f) if source == 0 and i == b else scaled(f) for i, f in enumerate(flags)]
            block(kvs[source], b * BLK, some, masks)

    masks = []
    some = 0
    for i in range(PLANES):
        flags = [seen(i, 0, order[b]) for b in range(PLANES)]
        some += flags[0] + flags[1] + flags[2] + flags[3]
        row = jnp.zeros((1, BLK), jnp.float32)
        for b in range(2 * PLANES):
            flag = flags[b if b < PLANES else OTHER[b - PLANES]]
            row = jnp.where(lane % 16 // 2 == b, flag.astype(jnp.float32), row)
        masks.append(lambda part, row=row: part * row)
    for b in range(PLANES):
        block(prompt, b * BLK, (some > 0) & (d >= 1), masks)
    for head in range(2):
        for i in range(PLANES):
            lo = head * SHARD + i * BLK
            total = jnp.sum(tot[lo : lo + BLK], axis=1, keepdims=True)
            part = (acc[lo : lo + BLK] / total).astype(jnp.bfloat16)
            lanes = slice(head * HD, (head + 1) * HD)
            ours[i * SLOTS : (i + 1) * SLOTS, lanes] = part[:SLOTS]
            j = OTHER[i]
            theirs[j * SLOTS : (j + 1) * SLOTS, lanes] = part[SLOTS:]


def attend(pattern, q2, kvs, prompt):
    return pl.pallas_call(
        attend_kernel,
        in_specs=[SMEM] + [VMEM] * 6,
        out_specs=[VMEM] * 2,
        out_shape=[jax.ShapeDtypeStruct((PLANES * SLOTS, 2 * HD), jnp.bfloat16)] * 2,
        scratch_shapes=[
            pltpu.VMEM((1024, HD), jnp.float32),
            pltpu.VMEM((1024, HD), jnp.float32),
        ],
        compiler_params=pltpu.CompilerParams(vmem_limit_bytes=VMEM_BYTES),
        name="attend",
    )(pattern, q2, *kvs, prompt)


def out_kernel(ours, theirs, w0, w1, own, near_o, near_b, far, buf, sems):
    tile = D // TILES

    def copies(n):
        cols = pl.ds(n * tile, tile)
        return [
            pltpu.make_async_copy(w.at[:, cols], buf.at[n, pl.ds(i * 2 * HD, 2 * HD)], sems.at[n, i])
            for i, w in enumerate((w0, w1))
        ]

    for n in range(TILES):
        for copy in copies(n):
            copy.start()
    rows = jnp.concatenate([ours[...], theirs[...]], axis=1)
    for n in range(TILES):
        for copy in copies(n):
            copy.wait()
        total = jnp.dot(rows, buf[n], preferred_element_type=jnp.float32)
        cols = slice(n * tile, (n + 1) * tile)
        own[:, cols] = total[:SLOTS]
        near_o[:, cols] = total[SLOTS : 2 * SLOTS].astype(jnp.bfloat16)
        near_b[:, cols] = total[2 * SLOTS : 3 * SLOTS]
        far[:, cols] = total[3 * SLOTS :].astype(jnp.bfloat16)


def project_out(ours, theirs, w_own, w_sib):
    hbm = pl.BlockSpec(memory_space=pltpu.HBM)
    return pl.pallas_call(
        out_kernel,
        in_specs=[VMEM] * 2 + [hbm] * 2,
        out_specs=[VMEM] * 4,
        out_shape=[
            jax.ShapeDtypeStruct((SLOTS, D), t)
            for t in (jnp.float32, jnp.bfloat16, jnp.float32, jnp.bfloat16)
        ],
        scratch_shapes=[
            pltpu.VMEM((TILES, 4 * HD, D // TILES), jnp.bfloat16),
            pltpu.SemaphoreType.DMA((TILES, 2)),
        ],
        compiler_params=pltpu.CompilerParams(vmem_limit_bytes=VMEM_BYTES),
        name="project_out",
    )(ours, theirs, *[pltpu.with_memory_space_constraint(w, pltpu.HBM) for w in (w_own, w_sib)])


def body(
    rollout_rows, pack_dest, lengths, pattern, norm_gain, w_query, w_key, w_value, w_out, post_gain
):
    bf16 = jnp.bfloat16
    n_dp = lax.axis_size("dp")
    d = lax.axis_index("dp")
    per_peer = SLOTS // n_dp
    order_ids = jnp.arange(SLOTS, dtype=jnp.int32)

    target_dev = pack_dest // SHARD
    target_slot = pack_dest % SLOTS
    before = (target_dev[:, None] == target_dev[None, :]) & (order_ids[None, :] < order_ids[:, None])
    send_pos = target_dev * per_peer + jnp.sum(before.astype(jnp.int32), axis=1)
    placer = order_ids[:, None] == send_pos[None, :]
    send_rows = jnp.dot(placer.astype(bf16), rollout_rows, preferred_element_type=jnp.float32).astype(bf16)
    send_slots = jnp.sum(jnp.where(placer, target_slot[None, :], 0), axis=1)
    send = jnp.concatenate(
        [send_rows, jnp.broadcast_to(send_slots.astype(bf16)[:, None], (SLOTS, HD))], axis=1
    )
    width = D + HD
    got = lax.all_to_all(send.reshape(n_dp, per_peer, width), "dp", 0, 0, tiled=True)

    core, order = plane_order()
    later, _ = lax.optimization_barrier((lengths, send))
    cos_a, sin_a, cos_c, sin_c = tables(later)

    first = send[:per_peer]
    piece = jnp.pad(first, ((0, 8 - per_peer), (0, 0)))
    column = [to(piece, OUT), to(piece, BACK), to(piece, FAR)]
    w_sib = to(w_out, SIB)

    got, w_sib, _ = lax.optimization_barrier((got, w_sib, cos_a))
    got = got.reshape(SLOTS, width)
    arrange = order_ids[:, None] == got[:, D].astype(jnp.int32)[None, :]
    packed = jnp.dot(arrange.astype(bf16), got[:, :D], preferred_element_type=jnp.float32).astype(bf16)
    normed = rms_scale(packed.astype(jnp.float32), norm_gain).astype(bf16)

    near_o = to(normed, OUT)
    near_b = to(normed, BACK)
    own_s = to(normed, SIB)

    column, _ = lax.optimization_barrier((column, normed))
    early = jnp.concatenate([first] + [c[:per_peer] for c in column], axis=0)
    early_kv = early_keys(lengths, early, to(early, SIB), norm_gain, w_key, w_value, n_dp)
    near_o, near_b, _ = lax.optimization_barrier((near_o, near_b, early_kv))
    far_own = to(near_o, OUT)
    near_os = to(near_b, SIB)
    near_bs = to(near_o, SIB)
    q_a, kv_a = project_near(
        normed, own_s, near_o, near_os, near_b, near_bs, w_query, w_key, w_value, cos_a, sin_a
    )
    early_kv, _ = lax.optimization_barrier((early_kv, kv_a))
    prompt = lax.all_to_all(early_kv, "dp", 0, 0, tiled=True)
    prompt = prompt.reshape(SHARD, 2 * HD)

    far_own, _ = lax.optimization_barrier((far_own, kv_a))
    far_s = to(far_own, SIB)
    q, kv = project_far(
        far_own, far_s, w_query, w_key, w_value, cos_c, sin_c, q_a, kv_a
    )
    kvs = [kv] + [
        lax.ppermute(kv, "dp", [(s, s + k) for s in range(n_dp - k)]) for k in (1, 2, 3)
    ]
    ours, theirs = attend(pattern, q, kvs, prompt)

    own, sum_o, sum_b, sum_far = project_out(ours, to(theirs, SIB), w_out, w_sib)
    from_far = to(sum_far, OUT)
    from_b = to(sum_o, BACK)
    from_o = to((sum_b + from_far.astype(jnp.float32)).astype(bf16), OUT)
    summed = own + from_b.astype(jnp.float32) + from_o.astype(jnp.float32)
    result = packed.astype(jnp.float32) + rms_scale(summed, post_gain)
    return result.astype(bf16)


def solution(mesh):
    placed = (
        P(("dp", "tensor"), None),
        P(("dp", "tensor")),
        P(),
        P("dp", None),
        P(),
        P(None, "tensor"),
        P(None, "tensor"),
        P(None, "tensor"),
        P("tensor", None),
        P(),
    )
    return jax.shard_map(
        body, mesh=mesh, in_specs=placed, out_specs=P(("dp", "tensor"), None), check_vma=False
    )
```

```python
import functools
import math

import jax
import jax.numpy as jnp
import numpy as np
from jax import lax
from jax.experimental import pallas as pl
from jax.experimental.pallas import tpu as pltpu
from jax.sharding import PartitionSpec as P

HD = 128
BLK = 128
D = 4608
SHARD = 512
SLOTS = 64
PLANES = 4

SOFT_CAP = 50.0
QUERY_SCALE = 1.0 / 12.0
ROPE_BASE = 10000.0
EPSILON = 1e-06

OUT = [(t, (t + (6 if t % 2 else 2)) % 8) for t in range(8)]
BACK = [(t, (t + (2 if t % 2 else 6)) % 8) for t in range(8)]
FAR = [(t, (t + 4) % 8) for t in range(8)]
SIB = [(t, t ^ 1) for t in range(8)]
VMEM_BYTES = 16 << 20
TILES = 6
OTHER = (0, 2, 1, 3)


SMEM = pl.BlockSpec(memory_space=pltpu.SMEM)
VMEM = pl.BlockSpec(memory_space=pltpu.VMEM)


def inverse_freq():
    half = HD // 2
    steps = np.arange(half, dtype=np.float32) * np.float32(2.0) / np.float32(HD)
    freq = np.power(np.float32(ROPE_BASE), -steps).astype(np.float32)
    return jnp.asarray(np.concatenate([freq, freq])[None, :])


def rope(row_ids, lengths, freq):
    bound = lengths[0]
    past = jnp.where(row_ids >= bound, lengths[0], 0)
    for i in range(1, lengths.shape[0]):
        bound = bound + lengths[i]
        past = past + jnp.where(row_ids >= bound, lengths[i], 0)
    place = jnp.where(row_ids < lengths[0], row_ids, lengths[0] + row_ids - past)
    angles = place.astype(jnp.float32) * freq
    lane = lax.broadcasted_iota(jnp.int32, row_ids.shape, 1)
    sine = jnp.sin(angles)
    return jnp.cos(angles), jnp.where(lane < HD // 2, -sine, sine)


def plane_order():
    t = lax.axis_index("tensor")
    plane = t // 2
    core = t % 2
    side = 1 - 2 * core
    return core, [plane] + [(plane + PLANES + k) % PLANES for k in (-side, side, 2)]


def tables_kernel(lengths, freq, cos_a, sin_a, cos_c, sin_c):
    core, order = plane_order()
    base = lax.axis_index("dp") * SHARD
    local = lax.broadcasted_iota(jnp.int32, (BLK, HD), 0) ^ (core * SLOTS)
    for i in range(PLANES):
        c, s = rope(base + order[i] * BLK + local, lengths, freq[...])
        if i < 3:
            cos_a[i * BLK : (i + 1) * BLK] = c
            sin_a[i * BLK : (i + 1) * BLK] = s
        else:
            cos_c[...] = c
            sin_c[...] = s


def tables(lengths):
    return pl.pallas_call(
        tables_kernel,
        in_specs=[SMEM, VMEM],
        out_specs=[VMEM] * 4,
        out_shape=[jax.ShapeDtypeStruct((n, HD), jnp.float32) for n in (384, 384, BLK, BLK)],
        compiler_params=pltpu.CompilerParams(vmem_limit_bytes=VMEM_BYTES),
        name="tables",
    )(lengths, inverse_freq())


def early_kernel(lengths, freq, own, sib, gain, wk, wv, out):
    core, order = plane_order()
    rows = jnp.concatenate([own[...], sib[...]], axis=0)
    x = rms_scale(rows[:, :D].astype(jnp.float32), gain[...]).astype(jnp.bfloat16)
    slot = rows[:, D:].astype(jnp.int32)
    index = lax.broadcasted_iota(jnp.int32, slot.shape, 0) // 2
    source = jnp.zeros_like(index)
    for i in range(2 * PLANES):
        source = jnp.where(index == i, early_source(i, core, order), source)
    c, s = rope(source * SLOTS + slot, lengths, freq[...])
    kv = jnp.dot(x, jnp.concatenate([wk[...], wv[...]], axis=1), preferred_element_type=jnp.float32)
    k = kv[:, :HD]
    k = k * c + pltpu.roll(k, HD // 2, 1) * s
    both = jnp.concatenate([k, kv[:, HD:]], axis=1).astype(jnp.bfloat16)
    out[...] = jnp.broadcast_to(both[None], out.shape)


def early_source(i, core, order):
    if i < PLANES:
        return 2 * order[i] + core
    return 2 * order[OTHER[i - PLANES]] + 1 - core


def early_keys(lengths, own, sib, gain, w_key, w_value, copies):
    return pl.pallas_call(
        early_kernel,
        in_specs=[SMEM] + [VMEM] * 6,
        out_specs=VMEM,
        out_shape=jax.ShapeDtypeStruct((copies, 2 * own.shape[0], 2 * HD), jnp.bfloat16),
        compiler_params=pltpu.CompilerParams(vmem_limit_bytes=VMEM_BYTES),
        name="early",
    )(lengths, inverse_freq(), own, sib, gain[None, :], w_key, w_value)


def rms_scale(values, gain):
    return values * lax.rsqrt(jnp.mean(values * values, axis=-1, keepdims=True) + EPSILON) * gain


def to(values, pairs):
    return lax.ppermute(values, "tensor", pairs)


def qkv(pieces, wq, wk, wv, cos, sin):
    x = jnp.concatenate([r[...] for r in pieces], axis=0)
    c = cos[...]
    s = sin[...]

    def turn(v):
        return (v * c + pltpu.roll(v, HD // 2, 1) * s).astype(jnp.bfloat16)

    q = jnp.dot(x, wq[...], preferred_element_type=jnp.float32)
    wkv = jnp.concatenate([wk[...], wv[...]], axis=1)
    kv = jnp.dot(x, wkv, preferred_element_type=jnp.float32)
    return turn(q[:, :HD]), turn(q[:, HD:]), turn(kv[:, :HD]), kv[:, HD:].astype(jnp.bfloat16)


def near_kernel(x0, x1, x2, x3, x4, x5, wq, wk, wv, cos, sin, q_out, kv_out):
    q0, q1, k, v = qkv((x0, x1, x2, x3, x4, x5), wq, wk, wv, cos, sin)
    q_out[0] = q0
    q_out[1] = q1
    kv_out[:, :HD] = k
    kv_out[:, HD:] = v


def far_kernel(x0, x1, wq, wk, wv, cos, sin, q_in, q_out, kv_out):
    q0, q1, k, v = qkv((x0, x1), wq, wk, wv, cos, sin)
    near = SHARD - BLK
    q_out[:near] = q_in[0]
    q_out[near:SHARD] = q0
    q_out[SHARD : SHARD + near] = q_in[1]
    q_out[SHARD + near :] = q1
    kv_out[:, :HD] = k
    kv_out[:, HD:] = v


def project_near(*args):
    rows = SHARD - BLK
    return pl.pallas_call(
        near_kernel,
        in_specs=[VMEM] * len(args),
        out_specs=[VMEM] * 2,
        out_shape=[
            jax.ShapeDtypeStruct((2, rows, HD), jnp.bfloat16),
            jax.ShapeDtypeStruct((rows, 2 * HD), jnp.bfloat16),
        ],
        compiler_params=pltpu.CompilerParams(vmem_limit_bytes=VMEM_BYTES),
        name="project_near",
    )(*args)


def project_far(*args):
    return pl.pallas_call(
        far_kernel,
        in_specs=[VMEM] * len(args),
        out_specs=[VMEM] * 2,
        out_shape=[
            jax.ShapeDtypeStruct((2 * SHARD, HD), jnp.bfloat16),
            jax.ShapeDtypeStruct((BLK, 2 * HD), jnp.bfloat16),
        ],
        compiler_params=pltpu.CompilerParams(vmem_limit_bytes=VMEM_BYTES),
        name="project_far",
    )(*args)


def attend_kernel(pattern, q2, *refs):
    kvs = refs[:8]
    prompt = refs[8]
    ours, theirs, acc, tot = refs[9:]
    acc[...] = jnp.zeros_like(acc)
    tot[...] = jnp.zeros_like(tot)
    core, order = plane_order()
    d = lax.axis_index("dp")
    lane = lax.broadcasted_iota(jnp.int32, (1, BLK), 1)

    def block(ref, row, some, masks):
        @pl.when(some)
        def _():
            k = ref[row : row + BLK, :HD]
            v = ref[row : row + BLK, HD:]
            scores = lax.dot_general(
                q2[...], k, (((1,), (1,)), ((), ())), preferred_element_type=jnp.float32
            )
            weights = jnp.exp2(jnp.tanh(scores * (QUERY_SCALE / SOFT_CAP)) * (SOFT_CAP * math.log2(math.e)))
            parts = []
            for i in range(2 * PLANES):
                parts.append(masks[i % PLANES](weights[i * BLK : (i + 1) * BLK]))
            weights = jnp.concatenate(parts, axis=0)
            tot[...] += weights
            acc[...] += jnp.dot(weights.astype(jnp.bfloat16), v, preferred_element_type=jnp.float32)

    def scaled(flag):
        return lambda part: part * flag.astype(jnp.float32)

    def causal(flag):
        def mask(part):
            flip = core * SLOTS
            rows_id = lax.broadcasted_iota(jnp.int32, (BLK, BLK), 0) ^ flip
            cols_id = lax.broadcasted_iota(jnp.int32, (BLK, BLK), 1) ^ flip
            return jnp.where(cols_id <= rows_id, part, 0.0) * flag.astype(jnp.float32)

        return mask

    def seen(i, shard, plane):
        return (pattern[order[i], shard * PLANES + plane] == 1).astype(jnp.int32)

    for source in range(4):
        shard = jnp.maximum(d - source, 0)
        for b in range(PLANES):
            flags = [seen(i, shard, order[b]) for i in range(PLANES)]
            some = flags[0] + flags[1] + flags[2] + flags[3] > 0
            if source:
                some = some & (d - source >= 1)
            masks = [causal(f) if source == 0 and i == b else scaled(f) for i, f in enumerate(flags)]
            ref, row = (kvs[2 * source], b * BLK) if b < 3 else (kvs[2 * source + 1], 0)
            block(ref, row, some, masks)

    masks = []
    some = 0
    for i in range(PLANES):
        flags = [seen(i, 0, order[b]) for b in range(PLANES)]
        some += flags[0] + flags[1] + flags[2] + flags[3]
        row = jnp.zeros((1, BLK), jnp.float32)
        for b in range(2 * PLANES):
            flag = flags[b if b < PLANES else OTHER[b - PLANES]]
            row = jnp.where(lane % 16 // 2 == b, flag.astype(jnp.float32), row)
        masks.append(lambda part, row=row: part * row)
    for b in range(PLANES):
        block(prompt, b * BLK, (some > 0) & (d >= 1), masks)
    for head in range(2):
        for i in range(PLANES):
            lo = head * SHARD + i * BLK
            total = jnp.sum(tot[lo : lo + BLK], axis=1, keepdims=True)
            part = (acc[lo : lo + BLK] / total).astype(jnp.bfloat16)
            lanes = slice(head * HD, (head + 1) * HD)
            ours[i * SLOTS : (i + 1) * SLOTS, lanes] = part[:SLOTS]
            j = OTHER[i]
            theirs[j * SLOTS : (j + 1) * SLOTS, lanes] = part[SLOTS:]


def attend(pattern, q2, kvs, prompt):
    return pl.pallas_call(
        attend_kernel,
        in_specs=[SMEM] + [VMEM] * 10,
        out_specs=[VMEM] * 2,
        out_shape=[jax.ShapeDtypeStruct((PLANES * SLOTS, 2 * HD), jnp.bfloat16)] * 2,
        scratch_shapes=[
            pltpu.VMEM((1024, HD), jnp.float32),
            pltpu.VMEM((1024, HD), jnp.float32),
        ],
        compiler_params=pltpu.CompilerParams(vmem_limit_bytes=VMEM_BYTES),
        name="attend",
    )(pattern, q2, *kvs, prompt)


def out_kernel(chunks, ours, theirs, w0, w1, first, second, buf, sems):
    tile = D // TILES

    def copies(n):
        cols = pl.ds(n * tile, tile)
        return [
            pltpu.make_async_copy(w.at[:, cols], buf.at[n, pl.ds(i * 2 * HD, 2 * HD)], sems.at[n, i])
            for i, w in enumerate((w0, w1))
        ]

    for n in range(TILES):
        for copy in copies(n):
            copy.start()
    rows = jnp.concatenate(
        [
            jnp.concatenate([r[c * SLOTS : (c + 1) * SLOTS] for r in (ours, theirs)], axis=1)
            for c in chunks
        ],
        axis=0,
    )
    for n in range(TILES):
        for copy in copies(n):
            copy.wait()
        total = jnp.dot(rows, buf[n], preferred_element_type=jnp.float32)
        cols = slice(n * tile, (n + 1) * tile)
        first[:, cols] = total[:SLOTS].astype(first.dtype)
        second[:, cols] = total[SLOTS:].astype(second.dtype)


def project_out(chunks, dtype, ours, theirs, w_own, w_sib):
    hbm = pl.BlockSpec(memory_space=pltpu.HBM)
    return pl.pallas_call(
        functools.partial(out_kernel, chunks),
        in_specs=[VMEM] * 2 + [hbm] * 2,
        out_specs=[VMEM] * 2,
        out_shape=[jax.ShapeDtypeStruct((SLOTS, D), dtype)] * 2,
        scratch_shapes=[
            pltpu.VMEM((TILES, 4 * HD, D // TILES), jnp.bfloat16),
            pltpu.SemaphoreType.DMA((TILES, 2)),
        ],
        compiler_params=pltpu.CompilerParams(vmem_limit_bytes=VMEM_BYTES),
        name="project_out",
    )(ours, theirs, *[pltpu.with_memory_space_constraint(w, pltpu.HBM) for w in (w_own, w_sib)])


def body(
    rollout_rows, pack_dest, lengths, pattern, norm_gain, w_query, w_key, w_value, w_out, post_gain
):
    bf16 = jnp.bfloat16
    n_dp = lax.axis_size("dp")
    d = lax.axis_index("dp")
    per_peer = SLOTS // n_dp
    order_ids = jnp.arange(SLOTS, dtype=jnp.int32)

    target_dev = pack_dest // SHARD
    target_slot = pack_dest % SLOTS
    before = (target_dev[:, None] == target_dev[None, :]) & (order_ids[None, :] < order_ids[:, None])
    send_pos = target_dev * per_peer + jnp.sum(before.astype(jnp.int32), axis=1)
    placer = order_ids[:, None] == send_pos[None, :]
    send_rows = jnp.dot(placer.astype(bf16), rollout_rows, preferred_element_type=jnp.float32).astype(bf16)
    send_slots = jnp.sum(jnp.where(placer, target_slot[None, :], 0), axis=1)
    send = jnp.concatenate(
        [send_rows, jnp.broadcast_to(send_slots.astype(bf16)[:, None], (SLOTS, HD))], axis=1
    )
    width = D + HD
    got = lax.all_to_all(send.reshape(n_dp, per_peer, width), "dp", 0, 0, tiled=True)

    core, order = plane_order()
    later, _ = lax.optimization_barrier((lengths, send))
    cos_a, sin_a, cos_c, sin_c = tables(later)

    first = send[:per_peer]
    piece = jnp.pad(first, ((0, 8 - per_peer), (0, 0)))
    column = [to(piece, OUT), to(piece, BACK), to(piece, FAR)]
    w_sib = to(w_out, SIB)

    got, w_sib, _ = lax.optimization_barrier((got, w_sib, cos_a))
    got = got.reshape(SLOTS, width)
    arrange = order_ids[:, None] == got[:, D].astype(jnp.int32)[None, :]
    packed = jnp.dot(arrange.astype(bf16), got[:, :D], preferred_element_type=jnp.float32).astype(bf16)
    normed = rms_scale(packed.astype(jnp.float32), norm_gain).astype(bf16)

    near_o = to(normed, OUT)
    near_b = to(normed, BACK)
    own_s = to(normed, SIB)

    column, _ = lax.optimization_barrier((column, normed))
    early = jnp.concatenate([first] + [c[:per_peer] for c in column], axis=0)
    early_kv = early_keys(lengths, early, to(early, SIB), norm_gain, w_key, w_value, n_dp)
    prompt = lax.all_to_all(early_kv, "dp", 0, 0, tiled=True)
    prompt = prompt.reshape(SHARD, 2 * HD)
    near_o, near_b, prompt = lax.optimization_barrier((near_o, near_b, prompt))
    far_own = to(near_o, OUT)
    near_os = to(near_b, SIB)
    near_bs = to(near_o, SIB)
    q_a, kv_a = project_near(
        normed, own_s, near_o, near_os, near_b, near_bs, w_query, w_key, w_value, cos_a, sin_a
    )
    shifts = [[(s, s + k) for s in range(n_dp - k)] for k in (1, 2, 3)]
    kvs_a = [kv_a] + [lax.ppermute(kv_a, "dp", shift) for shift in shifts]
    far_own, kvs_a = lax.optimization_barrier((far_own, kvs_a))
    far_s = to(far_own, SIB)
    q, kv_c = project_far(far_own, far_s, w_query, w_key, w_value, cos_c, sin_c, q_a)
    kvs_c = [kv_c] + [lax.ppermute(kv_c, "dp", shift) for shift in shifts]
    kvs = [x for pair in zip(kvs_a, kvs_c) for x in pair]
    ours, theirs = attend(pattern, q, kvs, prompt)

    theirs = to(theirs, SIB)
    sum_far, sum_o = project_out((3, 1), bf16, ours, theirs, w_out, w_sib)
    theirs, sum_far = lax.optimization_barrier((theirs, sum_far))
    own, sum_b = project_out((0, 2), jnp.float32, ours, theirs, w_out, w_sib)
    from_far = to(sum_far, OUT)
    from_b = to(sum_o, BACK)
    from_o = to((sum_b + from_far.astype(jnp.float32)).astype(bf16), OUT)
    summed = own + from_b.astype(jnp.float32) + from_o.astype(jnp.float32)
    result = packed.astype(jnp.float32) + rms_scale(summed, post_gain)
    return result.astype(bf16)


def solution(mesh):
    placed = (
        P(("dp", "tensor"), None),
        P(("dp", "tensor")),
        P(),
        P("dp", None),
        P(),
        P(None, "tensor"),
        P(None, "tensor"),
        P(None, "tensor"),
        P("tensor", None),
        P(),
    )
    return jax.shard_map(
        body, mesh=mesh, in_specs=placed, out_specs=P(("dp", "tensor"), None), check_vma=False
    )
```

```python
import functools
import math

import jax
import jax.numpy as jnp
import numpy as np
from jax import lax
from jax.experimental import pallas as pl
from jax.experimental.pallas import tpu as pltpu
from jax.sharding import PartitionSpec as P

HD = 128
BLK = 128
D = 4608
SHARD = 512
SLOTS = 64
PLANES = 4

SOFT_CAP = 50.0
QUERY_SCALE = 1.0 / 12.0
ROPE_BASE = 10000.0
EPSILON = 1e-06

OUT = [(t, (t + (6 if t % 2 else 2)) % 8) for t in range(8)]
BACK = [(t, (t + (2 if t % 2 else 6)) % 8) for t in range(8)]
FAR = [(t, (t + 4) % 8) for t in range(8)]
SIB = [(t, t ^ 1) for t in range(8)]
VMEM_BYTES = 16 << 20
TILES = 6
CHUNKS = 3
OTHER = (0, 2, 1, 3)


SMEM = pl.BlockSpec(memory_space=pltpu.SMEM)
VMEM = pl.BlockSpec(memory_space=pltpu.VMEM)


def inverse_freq():
    half = HD // 2
    steps = np.arange(half, dtype=np.float32) * np.float32(2.0) / np.float32(HD)
    freq = np.power(np.float32(ROPE_BASE), -steps).astype(np.float32)
    return jnp.asarray(np.concatenate([freq, freq])[None, :])


def rope(row_ids, lengths, freq):
    bound = lengths[0]
    past = jnp.where(row_ids >= bound, lengths[0], 0)
    for i in range(1, lengths.shape[0]):
        bound = bound + lengths[i]
        past = past + jnp.where(row_ids >= bound, lengths[i], 0)
    place = jnp.where(row_ids < lengths[0], row_ids, lengths[0] + row_ids - past)
    angles = place.astype(jnp.float32) * freq
    lane = lax.broadcasted_iota(jnp.int32, row_ids.shape, 1)
    sine = jnp.sin(angles)
    return jnp.cos(angles), jnp.where(lane < HD // 2, -sine, sine)


def plane_order():
    t = lax.axis_index("tensor")
    plane = t // 2
    core = t % 2
    side = 1 - 2 * core
    return core, [plane] + [(plane + PLANES + k) % PLANES for k in (-side, side, 2)]


def tables_kernel(lengths, freq, cos_a, sin_a, cos_c, sin_c):
    core, order = plane_order()
    base = lax.axis_index("dp") * SHARD
    local = lax.broadcasted_iota(jnp.int32, (BLK, HD), 0) ^ (core * SLOTS)
    for i in range(PLANES):
        c, s = rope(base + order[i] * BLK + local, lengths, freq[...])
        if i < 3:
            cos_a[i * BLK : (i + 1) * BLK] = c
            sin_a[i * BLK : (i + 1) * BLK] = s
        else:
            cos_c[...] = c
            sin_c[...] = s


def tables(lengths):
    return pl.pallas_call(
        tables_kernel,
        in_specs=[SMEM, VMEM],
        out_specs=[VMEM] * 4,
        out_shape=[jax.ShapeDtypeStruct((n, HD), jnp.float32) for n in (384, 384, BLK, BLK)],
        compiler_params=pltpu.CompilerParams(vmem_limit_bytes=VMEM_BYTES),
        name="tables",
    )(lengths, inverse_freq())


def early_kernel(lengths, freq, own, sib, gain, wk, wv, out):
    core, order = plane_order()
    rows = jnp.concatenate([own[...], sib[...]], axis=0)
    x = rms_scale(rows[:, :D].astype(jnp.float32), gain[...]).astype(jnp.bfloat16)
    slot = rows[:, D:].astype(jnp.int32)
    index = lax.broadcasted_iota(jnp.int32, slot.shape, 0) // 2
    source = jnp.zeros_like(index)
    for i in range(2 * PLANES):
        source = jnp.where(index == i, early_source(i, core, order), source)
    c, s = rope(source * SLOTS + slot, lengths, freq[...])
    kv = jnp.dot(x, jnp.concatenate([wk[...], wv[...]], axis=1), preferred_element_type=jnp.float32)
    k = kv[:, :HD]
    k = k * c + pltpu.roll(k, HD // 2, 1) * s
    both = jnp.concatenate([k, kv[:, HD:]], axis=1).astype(jnp.bfloat16)
    out[...] = jnp.broadcast_to(both[None], out.shape)


def early_source(i, core, order):
    if i < PLANES:
        return 2 * order[i] + core
    return 2 * order[OTHER[i - PLANES]] + 1 - core


def early_keys(lengths, own, sib, gain, w_key, w_value, copies):
    return pl.pallas_call(
        early_kernel,
        in_specs=[SMEM] + [VMEM] * 6,
        out_specs=VMEM,
        out_shape=jax.ShapeDtypeStruct((copies, 2 * own.shape[0], 2 * HD), jnp.bfloat16),
        compiler_params=pltpu.CompilerParams(vmem_limit_bytes=VMEM_BYTES),
        name="early",
    )(lengths, inverse_freq(), own, sib, gain[None, :], w_key, w_value)


def rms_scale(values, gain):
    return values * lax.rsqrt(jnp.mean(values * values, axis=-1, keepdims=True) + EPSILON) * gain


def to(values, pairs):
    return lax.ppermute(values, "tensor", pairs)


def turned(v, c, s):
    return (v * c + pltpu.roll(v, HD // 2, 1) * s).astype(jnp.bfloat16)


def near_kernel(x0, x1, x2, x3, x4, x5, wq, wk, wv, cos, sin, q_out, kv_out, buf, tab, sems):
    step = D // CHUNKS

    def copies(n):
        rows = pl.ds(n * step, step)
        return [
            pltpu.make_async_copy(w.at[rows], buf.at[rows, pl.ds(start, size)], sems.at[n, i])
            for i, (w, start, size) in enumerate(
                ((wq, 0, 2 * HD), (wk, 2 * HD, HD), (wv, 3 * HD, HD))
            )
        ]

    tables = [
        pltpu.make_async_copy(t, tab.at[i], sems.at[CHUNKS, i]) for i, t in enumerate((cos, sin))
    ]
    for n in range(CHUNKS):
        for copy in copies(n):
            copy.start()
    for copy in tables:
        copy.start()
    total = None
    for n in range(CHUNKS):
        for copy in copies(n):
            copy.wait()
        cols = slice(n * step, (n + 1) * step)
        x = jnp.concatenate([r[:, cols] for r in (x0, x1, x2, x3, x4, x5)], axis=0)
        part = jnp.dot(x, buf[cols], preferred_element_type=jnp.float32)
        total = part if total is None else total + part
    for copy in tables:
        copy.wait()
    c = tab[0]
    s = tab[1]
    q_out[0] = turned(total[:, :HD], c, s)
    q_out[1] = turned(total[:, HD : 2 * HD], c, s)
    kv_out[:, :HD] = turned(total[:, 2 * HD : 3 * HD], c, s)
    kv_out[:, HD:] = total[:, 3 * HD :].astype(jnp.bfloat16)


def far_kernel(x0, x1, wq, wk, wv, cos, sin, q_in, q_out, kv_out):
    x = jnp.concatenate([x0[...], x1[...]], axis=0)
    c = cos[...]
    s = sin[...]
    q = jnp.dot(x, wq[...], preferred_element_type=jnp.float32)
    wkv = jnp.concatenate([wk[...], wv[...]], axis=1)
    kv = jnp.dot(x, wkv, preferred_element_type=jnp.float32)
    q0 = turned(q[:, :HD], c, s)
    q1 = turned(q[:, HD:], c, s)
    k = turned(kv[:, :HD], c, s)
    v = kv[:, HD:].astype(jnp.bfloat16)
    near = SHARD - BLK
    q_out[:near] = q_in[0]
    q_out[near:SHARD] = q0
    q_out[SHARD : SHARD + near] = q_in[1]
    q_out[SHARD + near :] = q1
    kv_out[:, :HD] = k
    kv_out[:, HD:] = v


def project_near(*args):
    rows = SHARD - BLK
    hbm = pl.BlockSpec(memory_space=pltpu.HBM)
    rest = [pltpu.with_memory_space_constraint(a, pltpu.HBM) for a in args[6:]]
    return pl.pallas_call(
        near_kernel,
        in_specs=[VMEM] * 6 + [hbm] * 5,
        out_specs=[VMEM] * 2,
        out_shape=[
            jax.ShapeDtypeStruct((2, rows, HD), jnp.bfloat16),
            jax.ShapeDtypeStruct((rows, 2 * HD), jnp.bfloat16),
        ],
        scratch_shapes=[
            pltpu.VMEM((D, 4 * HD), jnp.bfloat16),
            pltpu.VMEM((2, rows, HD), jnp.float32),
            pltpu.SemaphoreType.DMA((CHUNKS + 1, 3)),
        ],
        compiler_params=pltpu.CompilerParams(vmem_limit_bytes=VMEM_BYTES),
        name="project_near",
    )(*args[:6], *rest)


def project_far(*args):
    return pl.pallas_call(
        far_kernel,
        in_specs=[VMEM] * len(args),
        out_specs=[VMEM] * 2,
        out_shape=[
            jax.ShapeDtypeStruct((2 * SHARD, HD), jnp.bfloat16),
            jax.ShapeDtypeStruct((BLK, 2 * HD), jnp.bfloat16),
        ],
        compiler_params=pltpu.CompilerParams(vmem_limit_bytes=VMEM_BYTES),
        name="project_far",
    )(*args)


def attend_kernel(pattern, q2, *refs):
    kvs = refs[:8]
    prompt = refs[8]
    ours, theirs, acc, tot = refs[9:]
    acc[...] = jnp.zeros_like(acc)
    tot[...] = jnp.zeros_like(tot)
    core, order = plane_order()
    d = lax.axis_index("dp")
    lane = lax.broadcasted_iota(jnp.int32, (1, BLK), 1)

    def block(ref, row, some, masks):
        @pl.when(some)
        def _():
            k = ref[row : row + BLK, :HD]
            v = ref[row : row + BLK, HD:]
            scores = lax.dot_general(
                q2[...], k, (((1,), (1,)), ((), ())), preferred_element_type=jnp.float32
            )
            weights = jnp.exp2(jnp.tanh(scores * (QUERY_SCALE / SOFT_CAP)) * (SOFT_CAP * math.log2(math.e)))
            parts = []
            for i in range(2 * PLANES):
                parts.append(masks[i % PLANES](weights[i * BLK : (i + 1) * BLK]))
            weights = jnp.concatenate(parts, axis=0)
            tot[...] += weights
            acc[...] += jnp.dot(weights.astype(jnp.bfloat16), v, preferred_element_type=jnp.float32)

    def scaled(flag):
        return lambda part: part * flag.astype(jnp.float32)

    def causal(flag):
        def mask(part):
            flip = core * SLOTS
            rows_id = lax.broadcasted_iota(jnp.int32, (BLK, BLK), 0) ^ flip
            cols_id = lax.broadcasted_iota(jnp.int32, (BLK, BLK), 1) ^ flip
            return jnp.where(cols_id <= rows_id, part, 0.0) * flag.astype(jnp.float32)

        return mask

    def seen(i, shard, plane):
        return (pattern[order[i], shard * PLANES + plane] == 1).astype(jnp.int32)

    for source in range(4):
        shard = jnp.maximum(d - source, 0)
        for b in range(PLANES):
            flags = [seen(i, shard, order[b]) for i in range(PLANES)]
            some = flags[0] + flags[1] + flags[2] + flags[3] > 0
            if source:
                some = some & (d - source >= 1)
            masks = [causal(f) if source == 0 and i == b else scaled(f) for i, f in enumerate(flags)]
            ref, row = (kvs[2 * source], b * BLK) if b < 3 else (kvs[2 * source + 1], 0)
            block(ref, row, some, masks)

    masks = []
    some = 0
    for i in range(PLANES):
        flags = [seen(i, 0, order[b]) for b in range(PLANES)]
        some += flags[0] + flags[1] + flags[2] + flags[3]
        row = jnp.zeros((1, BLK), jnp.float32)
        for b in range(2 * PLANES):
            flag = flags[b if b < PLANES else OTHER[b - PLANES]]
            row = jnp.where(lane % 16 // 2 == b, flag.astype(jnp.float32), row)
        masks.append(lambda part, row=row: part * row)
    for b in range(PLANES):
        block(prompt, b * BLK, (some > 0) & (d >= 1), masks)
    for head in range(2):
        for i in range(PLANES):
            lo = head * SHARD + i * BLK
            total = jnp.sum(tot[lo : lo + BLK], axis=1, keepdims=True)
            part = (acc[lo : lo + BLK] / total).astype(jnp.bfloat16)
            lanes = slice(head * HD, (head + 1) * HD)
            ours[i * SLOTS : (i + 1) * SLOTS, lanes] = part[:SLOTS]
            j = OTHER[i]
            theirs[j * SLOTS : (j + 1) * SLOTS, lanes] = part[SLOTS:]


def attend(pattern, q2, kvs, prompt):
    return pl.pallas_call(
        attend_kernel,
        in_specs=[SMEM] + [VMEM] * 10,
        out_specs=[VMEM] * 2,
        out_shape=[jax.ShapeDtypeStruct((PLANES * SLOTS, 2 * HD), jnp.bfloat16)] * 2,
        scratch_shapes=[
            pltpu.VMEM((1024, HD), jnp.float32),
            pltpu.VMEM((1024, HD), jnp.float32),
        ],
        compiler_params=pltpu.CompilerParams(vmem_limit_bytes=VMEM_BYTES),
        name="attend",
    )(pattern, q2, *kvs, prompt)


def out_kernel(chunks, ours, theirs, w0, w1, first, second, buf, sems):
    tile = D // TILES

    def copies(n):
        cols = pl.ds(n * tile, tile)
        return [
            pltpu.make_async_copy(w.at[:, cols], buf.at[n, pl.ds(i * 2 * HD, 2 * HD)], sems.at[n, i])
            for i, w in enumerate((w0, w1))
        ]

    for n in range(TILES):
        for copy in copies(n):
            copy.start()
    rows = jnp.concatenate(
        [
            jnp.concatenate([r[c * SLOTS : (c + 1) * SLOTS] for r in (ours, theirs)], axis=1)
            for c in chunks
        ],
        axis=0,
    )
    for n in range(TILES):
        for copy in copies(n):
            copy.wait()
        total = jnp.dot(rows, buf[n], preferred_element_type=jnp.float32)
        cols = slice(n * tile, (n + 1) * tile)
        first[:, cols] = total[:SLOTS].astype(first.dtype)
        second[:, cols] = total[SLOTS:].astype(second.dtype)


def project_out(chunks, dtype, ours, theirs, w_own, w_sib):
    hbm = pl.BlockSpec(memory_space=pltpu.HBM)
    return pl.pallas_call(
        functools.partial(out_kernel, chunks),
        in_specs=[VMEM] * 2 + [hbm] * 2,
        out_specs=[VMEM] * 2,
        out_shape=[jax.ShapeDtypeStruct((SLOTS, D), dtype)] * 2,
        scratch_shapes=[
            pltpu.VMEM((TILES, 4 * HD, D // TILES), jnp.bfloat16),
            pltpu.SemaphoreType.DMA((TILES, 2)),
        ],
        compiler_params=pltpu.CompilerParams(vmem_limit_bytes=VMEM_BYTES),
        name="project_out",
    )(ours, theirs, *[pltpu.with_memory_space_constraint(w, pltpu.HBM) for w in (w_own, w_sib)])


def body(
    rollout_rows, pack_dest, lengths, pattern, norm_gain, w_query, w_key, w_value, w_out, post_gain
):
    bf16 = jnp.bfloat16
    n_dp = lax.axis_size("dp")
    d = lax.axis_index("dp")
    per_peer = SLOTS // n_dp
    order_ids = jnp.arange(SLOTS, dtype=jnp.int32)

    target_dev = pack_dest // SHARD
    target_slot = pack_dest % SLOTS
    before = (target_dev[:, None] == target_dev[None, :]) & (order_ids[None, :] < order_ids[:, None])
    send_pos = target_dev * per_peer + jnp.sum(before.astype(jnp.int32), axis=1)
    placer = order_ids[:, None] == send_pos[None, :]
    send_rows = jnp.dot(placer.astype(bf16), rollout_rows, preferred_element_type=jnp.float32).astype(bf16)
    send_slots = jnp.sum(jnp.where(placer, target_slot[None, :], 0), axis=1)
    send = jnp.concatenate(
        [send_rows, jnp.broadcast_to(send_slots.astype(bf16)[:, None], (SLOTS, HD))], axis=1
    )
    width = D + HD
    got = lax.all_to_all(send.reshape(n_dp, per_peer, width), "dp", 0, 0, tiled=True)

    core, order = plane_order()
    later, _ = lax.optimization_barrier((lengths, send))
    cos_a, sin_a, cos_c, sin_c = tables(later)

    first = send[:per_peer]
    piece = jnp.pad(first, ((0, 8 - per_peer), (0, 0)))
    column = [to(piece, OUT), to(piece, BACK), to(piece, FAR)]
    w_sib = to(w_out, SIB)

    got, _ = lax.optimization_barrier((got, cos_a))
    got = got.reshape(SLOTS, width)
    arrange = order_ids[:, None] == got[:, D].astype(jnp.int32)[None, :]
    packed = jnp.dot(arrange.astype(bf16), got[:, :D], preferred_element_type=jnp.float32).astype(bf16)
    normed = rms_scale(packed.astype(jnp.float32), norm_gain).astype(bf16)

    near_o = to(normed, OUT)
    near_b = to(normed, BACK)
    own_s = to(normed, SIB)

    column, _ = lax.optimization_barrier((column, normed))
    early = jnp.concatenate([first] + [c[:per_peer] for c in column], axis=0)
    early_kv = early_keys(lengths, early, to(early, SIB), norm_gain, w_key, w_value, n_dp)
    prompt = lax.all_to_all(early_kv, "dp", 0, 0, tiled=True)
    prompt = prompt.reshape(SHARD, 2 * HD)
    near_o, near_b, prompt, w_sib = lax.optimization_barrier((near_o, near_b, prompt, w_sib))
    far_own = to(near_o, OUT)
    near_os = to(near_b, SIB)
    near_bs = to(near_o, SIB)
    q_a, kv_a = project_near(
        normed, own_s, near_o, near_os, near_b, near_bs, w_query, w_key, w_value, cos_a, sin_a
    )
    shifts = [[(s, s + k) for s in range(n_dp - k)] for k in (1, 2, 3)]
    kvs_a = [kv_a] + [lax.ppermute(kv_a, "dp", shift) for shift in shifts]
    far_own, kvs_a = lax.optimization_barrier((far_own, kvs_a))
    far_s = to(far_own, SIB)
    q, kv_c = project_far(far_own, far_s, w_query, w_key, w_value, cos_c, sin_c, q_a)
    kvs_c = [kv_c] + [lax.ppermute(kv_c, "dp", shift) for shift in shifts]
    kvs = [x for pair in zip(kvs_a, kvs_c) for x in pair]
    ours, theirs = attend(pattern, q, kvs, prompt)

    theirs = to(theirs, SIB)
    sum_far, sum_o = project_out((3, 1), bf16, ours, theirs, w_out, w_sib)
    theirs, sum_far = lax.optimization_barrier((theirs, sum_far))
    own, sum_b = project_out((0, 2), jnp.float32, ours, theirs, w_out, w_sib)
    from_far = to(sum_far, OUT)
    from_b = to(sum_o, BACK)
    from_o = to((sum_b + from_far.astype(jnp.float32)).astype(bf16), OUT)
    summed = own + from_b.astype(jnp.float32) + from_o.astype(jnp.float32)
    result = packed.astype(jnp.float32) + rms_scale(summed, post_gain)
    return result.astype(bf16)


def solution(mesh):
    placed = (
        P(("dp", "tensor"), None),
        P(("dp", "tensor")),
        P(),
        P("dp", None),
        P(),
        P(None, "tensor"),
        P(None, "tensor"),
        P(None, "tensor"),
        P("tensor", None),
        P(),
    )
    return jax.shard_map(
        body, mesh=mesh, in_specs=placed, out_specs=P(("dp", "tensor"), None), check_vma=False
    )
```

```python
import functools
import math

import jax
import jax.numpy as jnp
import numpy as np
from jax import lax
from jax.experimental import pallas as pl
from jax.experimental.pallas import tpu as pltpu
from jax.sharding import PartitionSpec as P

HD = 128
BLK = 128
D = 4608
SHARD = 512
SLOTS = 64
PLANES = 4

SOFT_CAP = 50.0
QUERY_SCALE = 1.0 / 12.0
ROPE_BASE = 10000.0
EPSILON = 1e-06

OUT = [(t, (t + (6 if t % 2 else 2)) % 8) for t in range(8)]
BACK = [(t, (t + (2 if t % 2 else 6)) % 8) for t in range(8)]
FAR = [(t, (t + 4) % 8) for t in range(8)]
SIB = [(t, t ^ 1) for t in range(8)]
VMEM_BYTES = 16 << 20
TILES = 6
CHUNKS = 3
OTHER = (0, 2, 1, 3)


SMEM = pl.BlockSpec(memory_space=pltpu.SMEM)
VMEM = pl.BlockSpec(memory_space=pltpu.VMEM)


def inverse_freq():
    half = HD // 2
    steps = np.arange(half, dtype=np.float32) * np.float32(2.0) / np.float32(HD)
    freq = np.power(np.float32(ROPE_BASE), -steps).astype(np.float32)
    return jnp.asarray(np.concatenate([freq, freq])[None, :])


def rope(row_ids, lengths, freq):
    bound = lengths[0]
    past = jnp.where(row_ids >= bound, lengths[0], 0)
    for i in range(1, lengths.shape[0]):
        bound = bound + lengths[i]
        past = past + jnp.where(row_ids >= bound, lengths[i], 0)
    place = jnp.where(row_ids < lengths[0], row_ids, lengths[0] + row_ids - past)
    angles = place.astype(jnp.float32) * freq
    lane = lax.broadcasted_iota(jnp.int32, row_ids.shape, 1)
    sine = jnp.sin(angles)
    return jnp.cos(angles), jnp.where(lane < HD // 2, -sine, sine)


def plane_order():
    t = lax.axis_index("tensor")
    plane = t // 2
    core = t % 2
    side = 1 - 2 * core
    return core, [plane] + [(plane + PLANES + k) % PLANES for k in (-side, side, 2)]


def tables_kernel(lengths, freq, cos_a, sin_a, cos_c, sin_c):
    core, order = plane_order()
    base = lax.axis_index("dp") * SHARD
    local = lax.broadcasted_iota(jnp.int32, (BLK, HD), 0) ^ (core * SLOTS)
    for i in range(PLANES):
        c, s = rope(base + order[i] * BLK + local, lengths, freq[...])
        if i < 3:
            cos_a[i * BLK : (i + 1) * BLK] = c
            sin_a[i * BLK : (i + 1) * BLK] = s
        else:
            cos_c[...] = c
            sin_c[...] = s


def tables(lengths):
    return pl.pallas_call(
        tables_kernel,
        in_specs=[SMEM, VMEM],
        out_specs=[VMEM] * 4,
        out_shape=[jax.ShapeDtypeStruct((n, HD), jnp.float32) for n in (384, 384, BLK, BLK)],
        compiler_params=pltpu.CompilerParams(vmem_limit_bytes=VMEM_BYTES),
        name="tables",
    )(lengths, inverse_freq())


def early_kernel(lengths, freq, own, sib, gain, wk, wv, out):
    core, order = plane_order()
    rows = jnp.concatenate([own[...], sib[...]], axis=0)
    x = rms_scale(rows[:, :D].astype(jnp.float32), gain[...]).astype(jnp.bfloat16)
    slot = rows[:, D:].astype(jnp.int32)
    index = lax.broadcasted_iota(jnp.int32, slot.shape, 0) // 2
    source = jnp.zeros_like(index)
    for i in range(2 * PLANES):
        source = jnp.where(index == i, early_source(i, core, order), source)
    c, s = rope(source * SLOTS + slot, lengths, freq[...])
    kv = jnp.dot(x, jnp.concatenate([wk[...], wv[...]], axis=1), preferred_element_type=jnp.float32)
    k = kv[:, :HD]
    k = k * c + pltpu.roll(k, HD // 2, 1) * s
    both = jnp.concatenate([k, kv[:, HD:]], axis=1).astype(jnp.bfloat16)
    out[...] = jnp.broadcast_to(both[None], out.shape)


def early_source(i, core, order):
    if i < PLANES:
        return 2 * order[i] + core
    return 2 * order[OTHER[i - PLANES]] + 1 - core


def early_keys(lengths, own, sib, gain, w_key, w_value, copies):
    return pl.pallas_call(
        early_kernel,
        in_specs=[SMEM] + [VMEM] * 6,
        out_specs=VMEM,
        out_shape=jax.ShapeDtypeStruct((copies, 2 * own.shape[0], 2 * HD), jnp.bfloat16),
        compiler_params=pltpu.CompilerParams(vmem_limit_bytes=VMEM_BYTES),
        name="early",
    )(lengths, inverse_freq(), own, sib, gain[None, :], w_key, w_value)


def rms_scale(values, gain):
    return values * lax.rsqrt(jnp.mean(values * values, axis=-1, keepdims=True) + EPSILON) * gain


def to(values, pairs):
    return lax.ppermute(values, "tensor", pairs)


def turned(v, c, s):
    return (v * c + pltpu.roll(v, HD // 2, 1) * s).astype(jnp.bfloat16)


def near_kernel(x0, x1, x2, x3, x4, x5, wq, wk, wv, cos, sin, q_out, kv_out, buf, tab, sems):
    step = D // CHUNKS

    def copies(n):
        rows = pl.ds(n * step, step)
        return [
            pltpu.make_async_copy(w.at[rows], buf.at[rows, pl.ds(start, size)], sems.at[n, i])
            for i, (w, start, size) in enumerate(
                ((wq, 0, 2 * HD), (wk, 2 * HD, HD), (wv, 3 * HD, HD))
            )
        ]

    tables = [
        pltpu.make_async_copy(t, tab.at[i], sems.at[CHUNKS, i]) for i, t in enumerate((cos, sin))
    ]
    for n in range(CHUNKS):
        for copy in copies(n):
            copy.start()
    for copy in tables:
        copy.start()
    total = None
    for n in range(CHUNKS):
        for copy in copies(n):
            copy.wait()
        cols = slice(n * step, (n + 1) * step)
        x = jnp.concatenate([r[:, cols] for r in (x0, x1, x2, x3, x4, x5)], axis=0)
        part = jnp.dot(x, buf[cols], preferred_element_type=jnp.float32)
        total = part if total is None else total + part
    for copy in tables:
        copy.wait()
    c = tab[0]
    s = tab[1]
    q_out[0] = turned(total[:, :HD], c, s)
    q_out[1] = turned(total[:, HD : 2 * HD], c, s)
    kv_out[:, :HD] = turned(total[:, 2 * HD : 3 * HD], c, s)
    kv_out[:, HD:] = total[:, 3 * HD :].astype(jnp.bfloat16)


def far_kernel(x0, x1, wq, wk, wv, cos, sin, q_in, q_out, kv_out):
    x = jnp.concatenate([x0[...], x1[...]], axis=0)
    c = cos[...]
    s = sin[...]
    q = jnp.dot(x, wq[...], preferred_element_type=jnp.float32)
    wkv = jnp.concatenate([wk[...], wv[...]], axis=1)
    kv = jnp.dot(x, wkv, preferred_element_type=jnp.float32)
    q0 = turned(q[:, :HD], c, s)
    q1 = turned(q[:, HD:], c, s)
    k = turned(kv[:, :HD], c, s)
    v = kv[:, HD:].astype(jnp.bfloat16)
    near = SHARD - BLK
    q_out[:near] = q_in[0]
    q_out[near:SHARD] = q0
    q_out[SHARD : SHARD + near] = q_in[1]
    q_out[SHARD + near :] = q1
    kv_out[:, :HD] = k
    kv_out[:, HD:] = v


def project_near(*args):
    rows = SHARD - BLK
    hbm = pl.BlockSpec(memory_space=pltpu.HBM)
    rest = [pltpu.with_memory_space_constraint(a, pltpu.HBM) for a in args[6:]]
    return pl.pallas_call(
        near_kernel,
        in_specs=[VMEM] * 6 + [hbm] * 5,
        out_specs=[VMEM] * 2,
        out_shape=[
            jax.ShapeDtypeStruct((2, rows, HD), jnp.bfloat16),
            jax.ShapeDtypeStruct((rows, 2 * HD), jnp.bfloat16),
        ],
        scratch_shapes=[
            pltpu.VMEM((D, 4 * HD), jnp.bfloat16),
            pltpu.VMEM((2, rows, HD), jnp.float32),
            pltpu.SemaphoreType.DMA((CHUNKS + 1, 3)),
        ],
        compiler_params=pltpu.CompilerParams(vmem_limit_bytes=VMEM_BYTES),
        name="project_near",
    )(*args[:6], *rest)


def project_far(*args):
    return pl.pallas_call(
        far_kernel,
        in_specs=[VMEM] * len(args),
        out_specs=[VMEM] * 2,
        out_shape=[
            jax.ShapeDtypeStruct((2 * SHARD, HD), jnp.bfloat16),
            jax.ShapeDtypeStruct((BLK, 2 * HD), jnp.bfloat16),
        ],
        compiler_params=pltpu.CompilerParams(vmem_limit_bytes=VMEM_BYTES),
        name="project_far",
    )(*args)


def attend_tile(q, blocks, acc, tot):
    some = blocks[0][2]
    for block in blocks[1:]:
        some = some | block[2]

    @pl.when(some)
    def _():
        k = jnp.concatenate([ref[row : row + BLK, :HD] for ref, row, _, _ in blocks], axis=0)
        v = jnp.concatenate([ref[row : row + BLK, HD:] for ref, row, _, _ in blocks], axis=0)
        scores = lax.dot_general(q[...], k, (((1,), (1,)), ((), ())), preferred_element_type=jnp.float32)
        weights = jnp.exp2(jnp.tanh(scores * (QUERY_SCALE / SOFT_CAP)) * (SOFT_CAP * math.log2(math.e)))
        rows = []
        for i in range(2 * PLANES):
            part = weights[i * BLK : (i + 1) * BLK]
            cols = [
                block[3][i % PLANES](part[:, j * BLK : (j + 1) * BLK]) for j, block in enumerate(blocks)
            ]
            rows.append(jnp.concatenate(cols, axis=1))
        weights = jnp.concatenate(rows, axis=0)
        sums = weights[:, :BLK]
        for j in range(1, len(blocks)):
            sums = sums + weights[:, j * BLK : (j + 1) * BLK]
        tot[...] += sums
        acc[...] += jnp.dot(weights.astype(jnp.bfloat16), v, preferred_element_type=jnp.float32)


def scaled(flag):
    return lambda part: part * flag.astype(jnp.float32)


def causal(flag, core):
    def mask(part):
        flip = core * SLOTS
        rows_id = lax.broadcasted_iota(jnp.int32, (BLK, BLK), 0) ^ flip
        cols_id = lax.broadcasted_iota(jnp.int32, (BLK, BLK), 1) ^ flip
        return jnp.where(cols_id <= rows_id, part, 0.0) * flag.astype(jnp.float32)

    return mask


def window_block(pattern, order, core, source, b, ref, row):
    d = lax.axis_index("dp")
    shard = jnp.maximum(d - source, 0)
    flags = [
        (pattern[order[i], shard * PLANES + order[b]] == 1).astype(jnp.int32) for i in range(PLANES)
    ]
    some = flags[0] + flags[1] + flags[2] + flags[3] > 0
    if source:
        some = some & (d - source >= 1)
        flags = [jnp.where(some, f, 0) for f in flags]
    masks = [causal(f, core) if source == 0 and i == b else scaled(f) for i, f in enumerate(flags)]
    return ref, row, some, masks


def attend_kernel(pattern, q, own_a, own_c, w1, w2, w3, prompt, acc, tot):
    acc[...] = jnp.zeros_like(acc)
    tot[...] = jnp.zeros_like(tot)
    core, order = plane_order()
    d = lax.axis_index("dp")
    lane = lax.broadcasted_iota(jnp.int32, (1, BLK), 1)

    def window(source, b, ref, row):
        return window_block(pattern, order, core, source, b, ref, row)

    attend_tile(q, [window(0, 0, own_a, 0), window(0, 1, own_a, BLK)], acc, tot)
    attend_tile(q, [window(0, 2, own_a, 2 * BLK), window(0, 3, own_c, 0)], acc, tot)
    for source, ref in ((1, w1), (2, w2), (3, w3)):
        attend_tile(q, [window(source, 0, ref, 0), window(source, 1, ref, BLK)], acc, tot)
    attend_tile(q, [window(1, 2, w1, 2 * BLK), window(2, 2, w2, 2 * BLK)], acc, tot)
    attend_tile(q, [window(3, 2, w3, 2 * BLK)], acc, tot)

    masks = []
    some = 0
    for i in range(PLANES):
        flags = [(pattern[order[i], order[b]] == 1).astype(jnp.int32) for b in range(PLANES)]
        some += flags[0] + flags[1] + flags[2] + flags[3]
        row = jnp.zeros((1, BLK), jnp.float32)
        for b in range(2 * PLANES):
            flag = flags[b if b < PLANES else OTHER[b - PLANES]]
            row = jnp.where(lane % 16 // 2 == b, flag.astype(jnp.float32), row)
        masks.append(lambda part, row=row: part * row)
    seen = (some > 0) & (d >= 1)
    for b in range(0, PLANES, 2):
        attend_tile(q, [(prompt, (b + j) * BLK, seen, masks) for j in range(2)], acc, tot)


def attend_far_kernel(pattern, q, w1, w2, w3, acc_in, tot_in, ours, theirs, acc, tot):
    acc[...] = acc_in[...]
    tot[...] = tot_in[...]
    core, order = plane_order()

    def window(source, ref):
        return window_block(pattern, order, core, source, 3, ref, 0)

    attend_tile(q, [window(1, w1), window(2, w2)], acc, tot)
    attend_tile(q, [window(3, w3)], acc, tot)
    for head in range(2):
        for i in range(PLANES):
            lo = head * SHARD + i * BLK
            total = jnp.sum(tot[lo : lo + BLK], axis=1, keepdims=True)
            part = (acc[lo : lo + BLK] / total).astype(jnp.bfloat16)
            lanes = slice(head * HD, (head + 1) * HD)
            ours[i * SLOTS : (i + 1) * SLOTS, lanes] = part[:SLOTS]
            j = OTHER[i]
            theirs[j * SLOTS : (j + 1) * SLOTS, lanes] = part[SLOTS:]


def attend(pattern, *args):
    return pl.pallas_call(
        attend_kernel,
        in_specs=[SMEM] + [VMEM] * len(args),
        out_specs=[VMEM] * 2,
        out_shape=[jax.ShapeDtypeStruct((2 * SHARD, HD), jnp.float32)] * 2,
        compiler_params=pltpu.CompilerParams(vmem_limit_bytes=VMEM_BYTES),
        name="attend",
    )(pattern, *args)


def attend_far(pattern, *args):
    return pl.pallas_call(
        attend_far_kernel,
        in_specs=[SMEM] + [VMEM] * len(args),
        out_specs=[VMEM] * 2,
        out_shape=[jax.ShapeDtypeStruct((PLANES * SLOTS, 2 * HD), jnp.bfloat16)] * 2,
        scratch_shapes=[pltpu.VMEM((2 * SHARD, HD), jnp.float32)] * 2,
        compiler_params=pltpu.CompilerParams(vmem_limit_bytes=VMEM_BYTES),
        name="attend_far",
    )(pattern, *args)


def out_kernel(chunks, ours, theirs, w0, w1, first, second, buf, sems):
    tile = D // TILES

    def copies(n):
        cols = pl.ds(n * tile, tile)
        return [
            pltpu.make_async_copy(w.at[:, cols], buf.at[n, pl.ds(i * 2 * HD, 2 * HD)], sems.at[n, i])
            for i, w in enumerate((w0, w1))
        ]

    for n in range(TILES):
        for copy in copies(n):
            copy.start()
    rows = jnp.concatenate(
        [
            jnp.concatenate([r[c * SLOTS : (c + 1) * SLOTS] for r in (ours, theirs)], axis=1)
            for c in chunks
        ],
        axis=0,
    )
    for n in range(TILES):
        for copy in copies(n):
            copy.wait()
        total = jnp.dot(rows, buf[n], preferred_element_type=jnp.float32)
        cols = slice(n * tile, (n + 1) * tile)
        first[:, cols] = total[:SLOTS].astype(first.dtype)
        second[:, cols] = total[SLOTS:].astype(second.dtype)


def project_out(chunks, dtype, ours, theirs, w_own, w_sib):
    hbm = pl.BlockSpec(memory_space=pltpu.HBM)
    return pl.pallas_call(
        functools.partial(out_kernel, chunks),
        in_specs=[VMEM] * 2 + [hbm] * 2,
        out_specs=[VMEM] * 2,
        out_shape=[jax.ShapeDtypeStruct((SLOTS, D), dtype)] * 2,
        scratch_shapes=[
            pltpu.VMEM((TILES, 4 * HD, D // TILES), jnp.bfloat16),
            pltpu.SemaphoreType.DMA((TILES, 2)),
        ],
        compiler_params=pltpu.CompilerParams(vmem_limit_bytes=VMEM_BYTES),
        name="project_out",
    )(ours, theirs, *[pltpu.with_memory_space_constraint(w, pltpu.HBM) for w in (w_own, w_sib)])


def body(
    rollout_rows, pack_dest, lengths, pattern, norm_gain, w_query, w_key, w_value, w_out, post_gain
):
    bf16 = jnp.bfloat16
    n_dp = lax.axis_size("dp")
    d = lax.axis_index("dp")
    per_peer = SLOTS // n_dp
    order_ids = jnp.arange(SLOTS, dtype=jnp.int32)

    target_dev = pack_dest // SHARD
    target_slot = pack_dest % SLOTS
    before = (target_dev[:, None] == target_dev[None, :]) & (order_ids[None, :] < order_ids[:, None])
    send_pos = target_dev * per_peer + jnp.sum(before.astype(jnp.int32), axis=1)
    placer = order_ids[:, None] == send_pos[None, :]
    send_rows = jnp.dot(placer.astype(bf16), rollout_rows, preferred_element_type=jnp.float32).astype(bf16)
    send_slots = jnp.sum(jnp.where(placer, target_slot[None, :], 0), axis=1)
    send = jnp.concatenate(
        [send_rows, jnp.broadcast_to(send_slots.astype(bf16)[:, None], (SLOTS, HD))], axis=1
    )
    width = D + HD
    got = lax.all_to_all(send.reshape(n_dp, per_peer, width), "dp", 0, 0, tiled=True)

    core, order = plane_order()
    later, _ = lax.optimization_barrier((lengths, send))
    cos_a, sin_a, cos_c, sin_c = tables(later)

    first = send[:per_peer]
    piece = jnp.pad(first, ((0, 8 - per_peer), (0, 0)))
    column = [to(piece, OUT), to(piece, BACK), to(piece, FAR)]
    w_sib = to(w_out, SIB)

    got, _ = lax.optimization_barrier((got, cos_a))
    got = got.reshape(SLOTS, width)
    arrange = order_ids[:, None] == got[:, D].astype(jnp.int32)[None, :]
    packed = jnp.dot(arrange.astype(bf16), got[:, :D], preferred_element_type=jnp.float32).astype(bf16)
    normed = rms_scale(packed.astype(jnp.float32), norm_gain).astype(bf16)

    near_o = to(normed, OUT)
    near_b = to(normed, BACK)
    own_s = to(normed, SIB)

    column, _ = lax.optimization_barrier((column, normed))
    early = jnp.concatenate([first] + [c[:per_peer] for c in column], axis=0)
    early_kv = early_keys(lengths, early, to(early, SIB), norm_gain, w_key, w_value, n_dp)
    prompt = lax.all_to_all(early_kv, "dp", 0, 0, tiled=True)
    prompt = prompt.reshape(SHARD, 2 * HD)
    near_o, near_b, prompt, w_sib = lax.optimization_barrier((near_o, near_b, prompt, w_sib))
    far_own = to(near_o, OUT)
    near_os = to(near_b, SIB)
    near_bs = to(near_o, SIB)
    q_a, kv_a = project_near(
        normed, own_s, near_o, near_os, near_b, near_bs, w_query, w_key, w_value, cos_a, sin_a
    )
    shifts = [[(s, s + k) for s in range(n_dp - k)] for k in (1, 2, 3)]
    kvs_a = [kv_a] + [lax.ppermute(kv_a, "dp", shift) for shift in shifts]
    far_own, kv_a = lax.optimization_barrier((far_own, kv_a))
    far_s = to(far_own, SIB)
    q, kv_c = project_far(far_own, far_s, w_query, w_key, w_value, cos_c, sin_c, q_a)
    kvs_c = [lax.ppermute(kv_c, "dp", shift) for shift in shifts]
    acc, tot = attend(pattern, q, kv_a, kv_c, *kvs_a[1:], prompt)
    ours, theirs = attend_far(pattern, q, *kvs_c, acc, tot)

    theirs = to(theirs, SIB)
    sum_far, sum_o = project_out((3, 1), bf16, ours, theirs, w_out, w_sib)
    theirs, sum_far = lax.optimization_barrier((theirs, sum_far))
    own, sum_b = project_out((0, 2), jnp.float32, ours, theirs, w_out, w_sib)
    from_far = to(sum_far, OUT)
    from_b = to(sum_o, BACK)
    from_o = to((sum_b + from_far.astype(jnp.float32)).astype(bf16), OUT)
    summed = own + from_b.astype(jnp.float32) + from_o.astype(jnp.float32)
    result = packed.astype(jnp.float32) + rms_scale(summed, post_gain)
    return result.astype(bf16)


def solution(mesh):
    placed = (
        P(("dp", "tensor"), None),
        P(("dp", "tensor")),
        P(),
        P("dp", None),
        P(),
        P(None, "tensor"),
        P(None, "tensor"),
        P(None, "tensor"),
        P("tensor", None),
        P(),
    )
    return jax.shard_map(
        body, mesh=mesh, in_specs=placed, out_specs=P(("dp", "tensor"), None), check_vma=False
    )
```

```python
import functools
import math

import jax
import jax.numpy as jnp
import numpy as np
from jax import lax
from jax.experimental import pallas as pl
from jax.experimental.pallas import tpu as pltpu
from jax.sharding import PartitionSpec as P

HD = 128
BLK = 128
D = 4608
SHARD = 512
SLOTS = 64
PLANES = 4

SOFT_CAP = 50.0
QUERY_SCALE = 1.0 / 12.0
ROPE_BASE = 10000.0
EPSILON = 1e-06

OUT = [(t, (t + (6 if t % 2 else 2)) % 8) for t in range(8)]
BACK = [(t, (t + (2 if t % 2 else 6)) % 8) for t in range(8)]
FAR = [(t, (t + 4) % 8) for t in range(8)]
SIB = [(t, t ^ 1) for t in range(8)]
VMEM_BYTES = 16 << 20
TILES = 6
CHUNKS = 3
OTHER = (0, 2, 1, 3)


SMEM = pl.BlockSpec(memory_space=pltpu.SMEM)
VMEM = pl.BlockSpec(memory_space=pltpu.VMEM)


def inverse_freq():
    half = HD // 2
    steps = np.arange(half, dtype=np.float32) * np.float32(2.0) / np.float32(HD)
    freq = np.power(np.float32(ROPE_BASE), -steps).astype(np.float32)
    return jnp.asarray(np.concatenate([freq, freq])[None, :])


def rope(row_ids, lengths, freq):
    bound = lengths[0]
    past = jnp.where(row_ids >= bound, lengths[0], 0)
    for i in range(1, lengths.shape[0]):
        bound = bound + lengths[i]
        past = past + jnp.where(row_ids >= bound, lengths[i], 0)
    place = jnp.where(row_ids < lengths[0], row_ids, lengths[0] + row_ids - past)
    angles = place.astype(jnp.float32) * freq
    lane = lax.broadcasted_iota(jnp.int32, row_ids.shape, 1)
    sine = jnp.sin(angles)
    return jnp.cos(angles), jnp.where(lane < HD // 2, -sine, sine)


def plane_order():
    t = lax.axis_index("tensor")
    plane = t // 2
    core = t % 2
    side = 1 - 2 * core
    return core, [plane] + [(plane + PLANES + k) % PLANES for k in (-side, side, 2)]


def tables_kernel(lengths, freq, cos_a, sin_a, cos_c, sin_c):
    core, order = plane_order()
    base = lax.axis_index("dp") * SHARD
    local = lax.broadcasted_iota(jnp.int32, (BLK, HD), 0) ^ (core * SLOTS)
    for i in range(PLANES):
        c, s = rope(base + order[i] * BLK + local, lengths, freq[...])
        if i < 3:
            cos_a[i * BLK : (i + 1) * BLK] = c
            sin_a[i * BLK : (i + 1) * BLK] = s
        else:
            cos_c[...] = c
            sin_c[...] = s


def tables(lengths):
    return pl.pallas_call(
        tables_kernel,
        in_specs=[SMEM, VMEM],
        out_specs=[VMEM] * 4,
        out_shape=[jax.ShapeDtypeStruct((n, HD), jnp.float32) for n in (384, 384, BLK, BLK)],
        compiler_params=pltpu.CompilerParams(vmem_limit_bytes=VMEM_BYTES),
        name="tables",
    )(lengths, inverse_freq())


def early_kernel(lengths, freq, own, sib, gain, wk, wv, out):
    core, order = plane_order()
    rows = jnp.concatenate([own[...], sib[...]], axis=0)
    x = rms_scale(rows[:, :D].astype(jnp.float32), gain[...]).astype(jnp.bfloat16)
    slot = rows[:, D:].astype(jnp.int32)
    index = lax.broadcasted_iota(jnp.int32, slot.shape, 0) // 2
    source = jnp.zeros_like(index)
    for i in range(2 * PLANES):
        source = jnp.where(index == i, early_source(i, core, order), source)
    c, s = rope(source * SLOTS + slot, lengths, freq[...])
    kv = jnp.dot(x, jnp.concatenate([wk[...], wv[...]], axis=1), preferred_element_type=jnp.float32)
    k = kv[:, :HD]
    k = k * c + pltpu.roll(k, HD // 2, 1) * s
    both = jnp.concatenate([k, kv[:, HD:]], axis=1).astype(jnp.bfloat16)
    out[...] = jnp.broadcast_to(both[None], out.shape)


def early_source(i, core, order):
    if i < PLANES:
        return 2 * order[i] + core
    return 2 * order[OTHER[i - PLANES]] + 1 - core


def early_keys(lengths, own, sib, gain, w_key, w_value, copies):
    return pl.pallas_call(
        early_kernel,
        in_specs=[SMEM] + [VMEM] * 6,
        out_specs=VMEM,
        out_shape=jax.ShapeDtypeStruct((copies, 2 * own.shape[0], 2 * HD), jnp.bfloat16),
        compiler_params=pltpu.CompilerParams(vmem_limit_bytes=VMEM_BYTES),
        name="early",
    )(lengths, inverse_freq(), own, sib, gain[None, :], w_key, w_value)


def rms_scale(values, gain):
    return values * lax.rsqrt(jnp.mean(values * values, axis=-1, keepdims=True) + EPSILON) * gain


def to(values, pairs):
    return lax.ppermute(values, "tensor", pairs)


def turned(v, c, s):
    return (v * c + pltpu.roll(v, HD // 2, 1) * s).astype(jnp.bfloat16)


def near_kernel(x0, x1, x2, x3, x4, x5, wq, wk, wv, cos, sin, q_out, kv_out, buf, tab, sems):
    step = D // CHUNKS

    def copies(n):
        rows = pl.ds(n * step, step)
        return [
            pltpu.make_async_copy(w.at[rows], buf.at[rows, pl.ds(start, size)], sems.at[n, i])
            for i, (w, start, size) in enumerate(
                ((wq, 0, 2 * HD), (wk, 2 * HD, HD), (wv, 3 * HD, HD))
            )
        ]

    tables = [
        pltpu.make_async_copy(t, tab.at[i], sems.at[CHUNKS, i]) for i, t in enumerate((cos, sin))
    ]
    for n in range(CHUNKS):
        for copy in copies(n):
            copy.start()
    for copy in tables:
        copy.start()
    total = None
    for n in range(CHUNKS):
        for copy in copies(n):
            copy.wait()
        cols = slice(n * step, (n + 1) * step)
        x = jnp.concatenate([r[:, cols] for r in (x0, x1, x2, x3, x4, x5)], axis=0)
        part = jnp.dot(x, buf[cols], preferred_element_type=jnp.float32)
        total = part if total is None else total + part
    for copy in tables:
        copy.wait()
    c = tab[0]
    s = tab[1]
    q_out[0] = turned(total[:, :HD], c, s)
    q_out[1] = turned(total[:, HD : 2 * HD], c, s)
    kv_out[:, :HD] = turned(total[:, 2 * HD : 3 * HD], c, s)
    kv_out[:, HD:] = total[:, 3 * HD :].astype(jnp.bfloat16)


def far_kernel(x0, x1, wq, wk, wv, cos, sin, q_in, q_out, kv_out):
    x = jnp.concatenate([x0[...], x1[...]], axis=0)
    c = cos[...]
    s = sin[...]
    q = jnp.dot(x, wq[...], preferred_element_type=jnp.float32)
    wkv = jnp.concatenate([wk[...], wv[...]], axis=1)
    kv = jnp.dot(x, wkv, preferred_element_type=jnp.float32)
    q0 = turned(q[:, :HD], c, s)
    q1 = turned(q[:, HD:], c, s)
    k = turned(kv[:, :HD], c, s)
    v = kv[:, HD:].astype(jnp.bfloat16)
    near = SHARD - BLK
    q_out[:near] = q_in[0]
    q_out[near:SHARD] = q0
    q_out[SHARD : SHARD + near] = q_in[1]
    q_out[SHARD + near :] = q1
    kv_out[:, :HD] = k
    kv_out[:, HD:] = v


def project_near(*args):
    rows = SHARD - BLK
    hbm = pl.BlockSpec(memory_space=pltpu.HBM)
    rest = [pltpu.with_memory_space_constraint(a, pltpu.HBM) for a in args[6:]]
    return pl.pallas_call(
        near_kernel,
        in_specs=[VMEM] * 6 + [hbm] * 5,
        out_specs=[VMEM] * 2,
        out_shape=[
            jax.ShapeDtypeStruct((2, rows, HD), jnp.bfloat16),
            jax.ShapeDtypeStruct((rows, 2 * HD), jnp.bfloat16),
        ],
        scratch_shapes=[
            pltpu.VMEM((D, 4 * HD), jnp.bfloat16),
            pltpu.VMEM((2, rows, HD), jnp.float32),
            pltpu.SemaphoreType.DMA((CHUNKS + 1, 3)),
        ],
        compiler_params=pltpu.CompilerParams(vmem_limit_bytes=VMEM_BYTES),
        name="project_near",
    )(*args[:6], *rest)


def project_far(*args):
    return pl.pallas_call(
        far_kernel,
        in_specs=[VMEM] * len(args),
        out_specs=[VMEM] * 2,
        out_shape=[
            jax.ShapeDtypeStruct((2 * SHARD, HD), jnp.bfloat16),
            jax.ShapeDtypeStruct((BLK, 2 * HD), jnp.bfloat16),
        ],
        compiler_params=pltpu.CompilerParams(vmem_limit_bytes=VMEM_BYTES),
        name="project_far",
    )(*args)


def attend_tile(q, blocks, acc, tot):
    some = blocks[0][2]
    for block in blocks[1:]:
        some = some | block[2]

    @pl.when(some)
    def _():
        k = jnp.concatenate([ref[row : row + BLK, :HD] for ref, row, _, _ in blocks], axis=0)
        v = jnp.concatenate([ref[row : row + BLK, HD:] for ref, row, _, _ in blocks], axis=0)
        scores = lax.dot_general(q[...], k, (((1,), (1,)), ((), ())), preferred_element_type=jnp.float32)
        weights = jnp.exp2(jnp.tanh(scores * (QUERY_SCALE / SOFT_CAP)) * (SOFT_CAP * math.log2(math.e)))
        rows = []
        for i in range(2 * PLANES):
            part = weights[i * BLK : (i + 1) * BLK]
            cols = [
                block[3][i % PLANES](part[:, j * BLK : (j + 1) * BLK]) for j, block in enumerate(blocks)
            ]
            rows.append(jnp.concatenate(cols, axis=1))
        weights = jnp.concatenate(rows, axis=0)
        sums = weights[:, :BLK]
        for j in range(1, len(blocks)):
            sums = sums + weights[:, j * BLK : (j + 1) * BLK]
        tot[...] += sums
        acc[...] += jnp.dot(weights.astype(jnp.bfloat16), v, preferred_element_type=jnp.float32)


def scaled(flag):
    return lambda part: part * flag.astype(jnp.float32)


def causal(flag, core):
    def mask(part):
        flip = core * SLOTS
        rows_id = lax.broadcasted_iota(jnp.int32, (BLK, BLK), 0) ^ flip
        cols_id = lax.broadcasted_iota(jnp.int32, (BLK, BLK), 1) ^ flip
        return jnp.where(cols_id <= rows_id, part, 0.0) * flag.astype(jnp.float32)

    return mask


def window_block(pattern, order, core, source, b, ref, row):
    d = lax.axis_index("dp")
    shard = jnp.maximum(d - source, 0)
    flags = [
        (pattern[order[i], shard * PLANES + order[b]] == 1).astype(jnp.int32) for i in range(PLANES)
    ]
    some = flags[0] + flags[1] + flags[2] + flags[3] > 0
    if source:
        some = some & (d - source >= 1)
        flags = [jnp.where(some, f, 0) for f in flags]
    masks = [causal(f, core) if source == 0 and i == b else scaled(f) for i, f in enumerate(flags)]
    return ref, row, some, masks


def attend_kernel(pattern, q, own_a, own_c, w1, w2, w3, prompt, acc, tot):
    acc[...] = jnp.zeros_like(acc)
    tot[...] = jnp.zeros_like(tot)
    core, order = plane_order()
    d = lax.axis_index("dp")
    lane = lax.broadcasted_iota(jnp.int32, (1, BLK), 1)

    def window(source, b, ref, row):
        return window_block(pattern, order, core, source, b, ref, row)

    attend_tile(q, [window(0, 0, own_a, 0), window(0, 1, own_a, BLK)], acc, tot)
    attend_tile(q, [window(0, 2, own_a, 2 * BLK), window(0, 3, own_c, 0)], acc, tot)
    for source, ref in ((1, w1), (2, w2), (3, w3)):
        attend_tile(q, [window(source, 0, ref, 0), window(source, 1, ref, BLK)], acc, tot)
    attend_tile(q, [window(1, 2, w1, 2 * BLK), window(2, 2, w2, 2 * BLK)], acc, tot)
    attend_tile(q, [window(3, 2, w3, 2 * BLK)], acc, tot)

    masks = []
    some = 0
    for i in range(PLANES):
        flags = [(pattern[order[i], order[b]] == 1).astype(jnp.int32) for b in range(PLANES)]
        some += flags[0] + flags[1] + flags[2] + flags[3]
        row = jnp.zeros((1, BLK), jnp.float32)
        for b in range(2 * PLANES):
            flag = flags[b if b < PLANES else OTHER[b - PLANES]]
            row = jnp.where(lane % 16 // 2 == b, flag.astype(jnp.float32), row)
        masks.append(lambda part, row=row: part * row)
    seen = (some > 0) & (d >= 1)
    for b in range(0, PLANES, 2):
        attend_tile(q, [(prompt, (b + j) * BLK, seen, masks) for j in range(2)], acc, tot)


def attend_far_kernel(pattern, q, w1, w2, w3, acc_in, tot_in, ours, theirs, acc, tot):
    acc[...] = acc_in[...]
    tot[...] = tot_in[...]
    core, order = plane_order()

    def window(source, ref):
        return window_block(pattern, order, core, source, 3, ref, 0)

    attend_tile(q, [window(1, w1), window(2, w2)], acc, tot)
    attend_tile(q, [window(3, w3)], acc, tot)
    for head in range(2):
        for i in range(PLANES):
            lo = head * SHARD + i * BLK
            total = jnp.sum(tot[lo : lo + BLK], axis=1, keepdims=True)
            part = (acc[lo : lo + BLK] / total).astype(jnp.bfloat16)
            lanes = slice(head * HD, (head + 1) * HD)
            ours[i * SLOTS : (i + 1) * SLOTS, lanes] = part[:SLOTS]
            j = OTHER[i]
            theirs[j * SLOTS : (j + 1) * SLOTS, lanes] = part[SLOTS:]


def attend(pattern, *args):
    return pl.pallas_call(
        attend_kernel,
        in_specs=[SMEM] + [VMEM] * len(args),
        out_specs=[VMEM] * 2,
        out_shape=[jax.ShapeDtypeStruct((2 * SHARD, HD), jnp.float32)] * 2,
        compiler_params=pltpu.CompilerParams(vmem_limit_bytes=VMEM_BYTES),
        name="attend",
    )(pattern, *args)


def attend_far(pattern, *args):
    return pl.pallas_call(
        attend_far_kernel,
        in_specs=[SMEM] + [VMEM] * len(args),
        out_specs=[VMEM] * 2,
        out_shape=[jax.ShapeDtypeStruct((PLANES * SLOTS, 2 * HD), jnp.bfloat16)] * 2,
        scratch_shapes=[pltpu.VMEM((2 * SHARD, HD), jnp.float32)] * 2,
        compiler_params=pltpu.CompilerParams(vmem_limit_bytes=VMEM_BYTES),
        name="attend_far",
    )(pattern, *args)


def out_kernel(chunks, ours, theirs, w0, w1, first, second, buf, sems):
    tile = D // TILES

    def copies(n):
        cols = pl.ds(n * tile, tile)
        return [
            pltpu.make_async_copy(w.at[:, cols], buf.at[n, pl.ds(i * 2 * HD, 2 * HD)], sems.at[n, i])
            for i, w in enumerate((w0, w1))
        ]

    for n in range(TILES):
        for copy in copies(n):
            copy.start()
    rows = jnp.concatenate(
        [
            jnp.concatenate([r[c * SLOTS : (c + 1) * SLOTS] for r in (ours, theirs)], axis=1)
            for c in chunks
        ],
        axis=0,
    )
    for n in range(TILES):
        for copy in copies(n):
            copy.wait()
        total = jnp.dot(rows, buf[n], preferred_element_type=jnp.float32)
        cols = slice(n * tile, (n + 1) * tile)
        first[:, cols] = total[:SLOTS].astype(first.dtype)
        second[:, cols] = total[SLOTS:].astype(second.dtype)


def project_out(chunks, dtype, ours, theirs, w_own, w_sib):
    hbm = pl.BlockSpec(memory_space=pltpu.HBM)
    return pl.pallas_call(
        functools.partial(out_kernel, chunks),
        in_specs=[VMEM] * 2 + [hbm] * 2,
        out_specs=[VMEM] * 2,
        out_shape=[jax.ShapeDtypeStruct((SLOTS, D), dtype)] * 2,
        scratch_shapes=[
            pltpu.VMEM((TILES, 4 * HD, D // TILES), jnp.bfloat16),
            pltpu.SemaphoreType.DMA((TILES, 2)),
        ],
        compiler_params=pltpu.CompilerParams(vmem_limit_bytes=VMEM_BYTES),
        name="project_out",
    )(ours, theirs, *[pltpu.with_memory_space_constraint(w, pltpu.HBM) for w in (w_own, w_sib)])


def body(
    rollout_rows, pack_dest, lengths, pattern, norm_gain, w_query, w_key, w_value, w_out, post_gain
):
    bf16 = jnp.bfloat16
    n_dp = lax.axis_size("dp")
    d = lax.axis_index("dp")
    per_peer = SLOTS // n_dp
    order_ids = jnp.arange(SLOTS, dtype=jnp.int32)

    target_dev = pack_dest // SHARD
    target_slot = pack_dest % SLOTS
    before = (target_dev[:, None] == target_dev[None, :]) & (order_ids[None, :] < order_ids[:, None])
    send_pos = target_dev * per_peer + jnp.sum(before.astype(jnp.int32), axis=1)
    placer = order_ids[:, None] == send_pos[None, :]
    send_rows = jnp.dot(placer.astype(bf16), rollout_rows, preferred_element_type=jnp.float32).astype(bf16)
    send_slots = jnp.sum(jnp.where(placer, target_slot[None, :], 0), axis=1)
    send = jnp.concatenate(
        [send_rows, jnp.broadcast_to(send_slots.astype(bf16)[:, None], (SLOTS, HD))], axis=1
    )
    width = D + HD
    got = lax.all_to_all(send.reshape(n_dp, per_peer, width), "dp", 0, 0, tiled=True)

    core, order = plane_order()
    first = send[:per_peer]
    piece = jnp.pad(first, ((0, 8 - per_peer), (0, 0)))
    column = [to(piece, OUT), to(piece, BACK), to(piece, FAR)]

    got = got.reshape(SLOTS, width)
    arrange = order_ids[:, None] == got[:, D].astype(jnp.int32)[None, :]
    packed = jnp.dot(arrange.astype(bf16), got[:, :D], preferred_element_type=jnp.float32).astype(bf16)
    packed = lax.optimization_barrier(packed)
    normed = rms_scale(packed.astype(jnp.float32), norm_gain).astype(bf16)

    near_o = to(normed, OUT)
    near_b = to(normed, BACK)
    own_s = to(normed, SIB)

    column, later, _ = lax.optimization_barrier((column, lengths, normed))
    cos_a, sin_a, cos_c, sin_c = tables(later)
    w_sib = to(w_out, SIB)
    early = jnp.concatenate([first] + [c[:per_peer] for c in column], axis=0)
    early_kv = early_keys(lengths, early, to(early, SIB), norm_gain, w_key, w_value, n_dp)
    prompt = lax.all_to_all(early_kv, "dp", 0, 0, tiled=True)
    prompt = prompt.reshape(SHARD, 2 * HD)
    near_o, near_b, prompt, w_sib, cos_a = lax.optimization_barrier(
        (near_o, near_b, prompt, w_sib, cos_a)
    )
    far_own = to(near_o, OUT)
    near_os = to(near_b, SIB)
    near_bs = to(near_o, SIB)
    q_a, kv_a = project_near(
        normed, own_s, near_o, near_os, near_b, near_bs, w_query, w_key, w_value, cos_a, sin_a
    )
    shifts = [[(s, s + k) for s in range(n_dp - k)] for k in (1, 2, 3)]
    kvs_a = [kv_a] + [lax.ppermute(kv_a, "dp", shift) for shift in shifts]
    far_own, kv_a = lax.optimization_barrier((far_own, kv_a))
    far_s = to(far_own, SIB)
    q, kv_c = project_far(far_own, far_s, w_query, w_key, w_value, cos_c, sin_c, q_a)
    kvs_c = [lax.ppermute(kv_c, "dp", shift) for shift in shifts]
    acc, tot = attend(pattern, q, kv_a, kv_c, *kvs_a[1:], prompt)
    ours, theirs = attend_far(pattern, q, *kvs_c, acc, tot)

    theirs = to(theirs, SIB)
    sum_far, sum_o = project_out((3, 1), bf16, ours, theirs, w_out, w_sib)
    theirs, sum_far = lax.optimization_barrier((theirs, sum_far))
    own, sum_b = project_out((0, 2), jnp.float32, ours, theirs, w_out, w_sib)
    from_far = to(sum_far, OUT)
    from_b = to(sum_o, BACK)
    from_o = to((sum_b + from_far.astype(jnp.float32)).astype(bf16), OUT)
    summed = own + from_b.astype(jnp.float32) + from_o.astype(jnp.float32)
    result = packed.astype(jnp.float32) + rms_scale(summed, post_gain)
    return result.astype(bf16)


def solution(mesh):
    placed = (
        P(("dp", "tensor"), None),
        P(("dp", "tensor")),
        P(),
        P("dp", None),
        P(),
        P(None, "tensor"),
        P(None, "tensor"),
        P(None, "tensor"),
        P("tensor", None),
        P(),
    )
    return jax.shard_map(
        body, mesh=mesh, in_specs=placed, out_specs=P(("dp", "tensor"), None), check_vma=False
    )
```

```python
import functools
import math

import jax
import jax.numpy as jnp
import numpy as np
from jax import lax
from jax.experimental import pallas as pl
from jax.experimental.pallas import tpu as pltpu
from jax.sharding import PartitionSpec as P

HD = 128
BLK = 128
D = 4608
SHARD = 512
SLOTS = 64
PLANES = 4

SOFT_CAP = 50.0
QUERY_SCALE = 1.0 / 12.0
ROPE_BASE = 10000.0
EPSILON = 1e-06

OUT = [(t, (t + (6 if t % 2 else 2)) % 8) for t in range(8)]
BACK = [(t, (t + (2 if t % 2 else 6)) % 8) for t in range(8)]
FAR = [(t, (t + 4) % 8) for t in range(8)]
SIB = [(t, t ^ 1) for t in range(8)]
VMEM_BYTES = 16 << 20
TILES = 6
CHUNKS = 3
OTHER = (0, 2, 1, 3)


SMEM = pl.BlockSpec(memory_space=pltpu.SMEM)
VMEM = pl.BlockSpec(memory_space=pltpu.VMEM)


def inverse_freq():
    half = HD // 2
    steps = np.arange(half, dtype=np.float32) * np.float32(2.0) / np.float32(HD)
    freq = np.power(np.float32(ROPE_BASE), -steps).astype(np.float32)
    return jnp.asarray(np.concatenate([freq, freq])[None, :])


def rope(row_ids, lengths, freq):
    bound = lengths[0]
    past = jnp.where(row_ids >= bound, lengths[0], 0)
    for i in range(1, lengths.shape[0]):
        bound = bound + lengths[i]
        past = past + jnp.where(row_ids >= bound, lengths[i], 0)
    place = jnp.where(row_ids < lengths[0], row_ids, lengths[0] + row_ids - past)
    angles = place.astype(jnp.float32) * freq
    lane = lax.broadcasted_iota(jnp.int32, row_ids.shape, 1)
    sine = jnp.sin(angles)
    return jnp.cos(angles), jnp.where(lane < HD // 2, -sine, sine)


def plane_order():
    t = lax.axis_index("tensor")
    plane = t // 2
    core = t % 2
    side = 1 - 2 * core
    return core, [plane] + [(plane + PLANES + k) % PLANES for k in (-side, side, 2)]


def tables_kernel(lengths, freq, cos_a, sin_a, cos_c, sin_c):
    core, order = plane_order()
    base = lax.axis_index("dp") * SHARD
    local = lax.broadcasted_iota(jnp.int32, (BLK, HD), 0) ^ (core * SLOTS)
    for i in range(PLANES):
        c, s = rope(base + order[i] * BLK + local, lengths, freq[...])
        if i < 3:
            cos_a[i * BLK : (i + 1) * BLK] = c
            sin_a[i * BLK : (i + 1) * BLK] = s
        else:
            cos_c[...] = c
            sin_c[...] = s


def tables(lengths):
    return pl.pallas_call(
        tables_kernel,
        in_specs=[SMEM, VMEM],
        out_specs=[VMEM] * 4,
        out_shape=[jax.ShapeDtypeStruct((n, HD), jnp.float32) for n in (384, 384, BLK, BLK)],
        compiler_params=pltpu.CompilerParams(vmem_limit_bytes=VMEM_BYTES),
        name="tables",
    )(lengths, inverse_freq())


def early_kernel(lengths, freq, own, sib, gain, wk, wv, out):
    core, order = plane_order()
    rows = jnp.concatenate([own[...], sib[...]], axis=0)
    x = rms_scale(rows[:, :D].astype(jnp.float32), gain[...]).astype(jnp.bfloat16)
    slot = rows[:, D:].astype(jnp.int32)
    index = lax.broadcasted_iota(jnp.int32, slot.shape, 0) // 2
    source = jnp.zeros_like(index)
    for i in range(2 * PLANES):
        source = jnp.where(index == i, early_source(i, core, order), source)
    c, s = rope(source * SLOTS + slot, lengths, freq[...])
    kv = jnp.dot(x, jnp.concatenate([wk[...], wv[...]], axis=1), preferred_element_type=jnp.float32)
    k = kv[:, :HD]
    k = k * c + pltpu.roll(k, HD // 2, 1) * s
    both = jnp.concatenate([k, kv[:, HD:]], axis=1).astype(jnp.bfloat16)
    out[...] = jnp.broadcast_to(both[None], out.shape)


def early_source(i, core, order):
    if i < PLANES:
        return 2 * order[i] + core
    return 2 * order[OTHER[i - PLANES]] + 1 - core


def early_keys(lengths, own, sib, gain, w_key, w_value, copies):
    return pl.pallas_call(
        early_kernel,
        in_specs=[SMEM] + [VMEM] * 6,
        out_specs=VMEM,
        out_shape=jax.ShapeDtypeStruct((copies, 2 * own.shape[0], 2 * HD), jnp.bfloat16),
        compiler_params=pltpu.CompilerParams(vmem_limit_bytes=VMEM_BYTES),
        name="early",
    )(lengths, inverse_freq(), own, sib, gain[None, :], w_key, w_value)


def rms_scale(values, gain):
    return values * lax.rsqrt(jnp.mean(values * values, axis=-1, keepdims=True) + EPSILON) * gain


def to(values, pairs):
    return lax.ppermute(values, "tensor", pairs)


def turned(v, c, s):
    return (v * c + pltpu.roll(v, HD // 2, 1) * s).astype(jnp.bfloat16)


def near_kernel(x0, x1, x2, x3, x4, x5, wq, wk, wv, cos, sin, q_out, kv_out, buf, tab, sems):
    step = D // CHUNKS

    def copies(n):
        rows = pl.ds(n * step, step)
        return [
            pltpu.make_async_copy(w.at[rows], buf.at[rows, pl.ds(start, size)], sems.at[n, i])
            for i, (w, start, size) in enumerate(
                ((wq, 0, 2 * HD), (wk, 2 * HD, HD), (wv, 3 * HD, HD))
            )
        ]

    tables = [
        pltpu.make_async_copy(t, tab.at[i], sems.at[CHUNKS, i]) for i, t in enumerate((cos, sin))
    ]
    for n in range(CHUNKS):
        for copy in copies(n):
            copy.start()
    for copy in tables:
        copy.start()
    total = None
    for n in range(CHUNKS):
        for copy in copies(n):
            copy.wait()
        cols = slice(n * step, (n + 1) * step)
        x = jnp.concatenate([r[:, cols] for r in (x0, x1, x2, x3, x4, x5)], axis=0)
        part = jnp.dot(x, buf[cols], preferred_element_type=jnp.float32)
        total = part if total is None else total + part
    for copy in tables:
        copy.wait()
    c = tab[0]
    s = tab[1]
    q_out[0] = turned(total[:, :HD], c, s)
    q_out[1] = turned(total[:, HD : 2 * HD], c, s)
    kv_out[:, :HD] = turned(total[:, 2 * HD : 3 * HD], c, s)
    kv_out[:, HD:] = total[:, 3 * HD :].astype(jnp.bfloat16)


def far_kernel(x0, x1, wq, wk, wv, cos, sin, q_in, q_out, kv_out):
    x = jnp.concatenate([x0[...], x1[...]], axis=0)
    c = cos[...]
    s = sin[...]
    q = jnp.dot(x, wq[...], preferred_element_type=jnp.float32)
    wkv = jnp.concatenate([wk[...], wv[...]], axis=1)
    kv = jnp.dot(x, wkv, preferred_element_type=jnp.float32)
    q0 = turned(q[:, :HD], c, s)
    q1 = turned(q[:, HD:], c, s)
    k = turned(kv[:, :HD], c, s)
    v = kv[:, HD:].astype(jnp.bfloat16)
    near = SHARD - BLK
    q_out[:near] = q_in[0]
    q_out[near:SHARD] = q0
    q_out[SHARD : SHARD + near] = q_in[1]
    q_out[SHARD + near :] = q1
    kv_out[:, :HD] = k
    kv_out[:, HD:] = v


def project_near(*args):
    rows = SHARD - BLK
    hbm = pl.BlockSpec(memory_space=pltpu.HBM)
    rest = [pltpu.with_memory_space_constraint(a, pltpu.HBM) for a in args[6:]]
    return pl.pallas_call(
        near_kernel,
        in_specs=[VMEM] * 6 + [hbm] * 5,
        out_specs=[VMEM] * 2,
        out_shape=[
            jax.ShapeDtypeStruct((2, rows, HD), jnp.bfloat16),
            jax.ShapeDtypeStruct((rows, 2 * HD), jnp.bfloat16),
        ],
        scratch_shapes=[
            pltpu.VMEM((D, 4 * HD), jnp.bfloat16),
            pltpu.VMEM((2, rows, HD), jnp.float32),
            pltpu.SemaphoreType.DMA((CHUNKS + 1, 3)),
        ],
        compiler_params=pltpu.CompilerParams(vmem_limit_bytes=VMEM_BYTES),
        name="project_near",
    )(*args[:6], *rest)


def project_far(*args):
    return pl.pallas_call(
        far_kernel,
        in_specs=[VMEM] * len(args),
        out_specs=[VMEM] * 2,
        out_shape=[
            jax.ShapeDtypeStruct((2 * SHARD, HD), jnp.bfloat16),
            jax.ShapeDtypeStruct((BLK, 2 * HD), jnp.bfloat16),
        ],
        compiler_params=pltpu.CompilerParams(vmem_limit_bytes=VMEM_BYTES),
        name="project_far",
    )(*args)


def attend_tile(q, blocks, acc, tot):
    some = blocks[0][2]
    for block in blocks[1:]:
        some = some | block[2]

    @pl.when(some)
    def _():
        k = jnp.concatenate([ref[row : row + BLK, :HD] for ref, row, _, _ in blocks], axis=0)
        v = jnp.concatenate([ref[row : row + BLK, HD:] for ref, row, _, _ in blocks], axis=0)
        scores = lax.dot_general(q[...], k, (((1,), (1,)), ((), ())), preferred_element_type=jnp.float32)
        weights = jnp.exp2(jnp.tanh(scores * (QUERY_SCALE / SOFT_CAP)) * (SOFT_CAP * math.log2(math.e)))
        rows = []
        for i in range(2 * PLANES):
            part = weights[i * BLK : (i + 1) * BLK]
            cols = [
                block[3][i % PLANES](part[:, j * BLK : (j + 1) * BLK]) for j, block in enumerate(blocks)
            ]
            rows.append(jnp.concatenate(cols, axis=1))
        weights = jnp.concatenate(rows, axis=0)
        sums = weights[:, :BLK]
        for j in range(1, len(blocks)):
            sums = sums + weights[:, j * BLK : (j + 1) * BLK]
        tot[...] += sums
        acc[...] += jnp.dot(weights.astype(jnp.bfloat16), v, preferred_element_type=jnp.float32)


def scaled(flag):
    return lambda part: part * flag.astype(jnp.float32)


def causal(flag, core):
    def mask(part):
        flip = core * SLOTS
        rows_id = lax.broadcasted_iota(jnp.int32, (BLK, BLK), 0) ^ flip
        cols_id = lax.broadcasted_iota(jnp.int32, (BLK, BLK), 1) ^ flip
        return jnp.where(cols_id <= rows_id, part, 0.0) * flag.astype(jnp.float32)

    return mask


def window_block(pattern, order, core, source, b, ref, row):
    d = lax.axis_index("dp")
    shard = jnp.maximum(d - source, 0)
    flags = [
        (pattern[order[i], shard * PLANES + order[b]] == 1).astype(jnp.int32) for i in range(PLANES)
    ]
    some = flags[0] + flags[1] + flags[2] + flags[3] > 0
    if source:
        some = some & (d - source >= 1)
        flags = [jnp.where(some, f, 0) for f in flags]
    masks = [causal(f, core) if source == 0 and i == b else scaled(f) for i, f in enumerate(flags)]
    return ref, row, some, masks


def attend_kernel(pattern, q, own_a, own_c, w1, w2, w3, prompt, acc, tot):
    acc[...] = jnp.zeros_like(acc)
    tot[...] = jnp.zeros_like(tot)
    core, order = plane_order()
    d = lax.axis_index("dp")
    lane = lax.broadcasted_iota(jnp.int32, (1, BLK), 1)

    def window(source, b, ref, row):
        return window_block(pattern, order, core, source, b, ref, row)

    attend_tile(q, [window(0, 0, own_a, 0), window(0, 1, own_a, BLK)], acc, tot)
    attend_tile(q, [window(0, 2, own_a, 2 * BLK), window(0, 3, own_c, 0)], acc, tot)
    for source, ref in ((1, w1), (2, w2), (3, w3)):
        attend_tile(q, [window(source, 0, ref, 0), window(source, 1, ref, BLK)], acc, tot)
    attend_tile(q, [window(1, 2, w1, 2 * BLK), window(2, 2, w2, 2 * BLK)], acc, tot)
    attend_tile(q, [window(3, 2, w3, 2 * BLK)], acc, tot)

    masks = []
    some = 0
    for i in range(PLANES):
        flags = [(pattern[order[i], order[b]] == 1).astype(jnp.int32) for b in range(PLANES)]
        some += flags[0] + flags[1] + flags[2] + flags[3]
        row = jnp.zeros((1, BLK), jnp.float32)
        for b in range(2 * PLANES):
            flag = flags[b if b < PLANES else OTHER[b - PLANES]]
            row = jnp.where(lane % 16 // 2 == b, flag.astype(jnp.float32), row)
        masks.append(lambda part, row=row: part * row)
    seen = (some > 0) & (d >= 1)
    for b in range(0, PLANES, 2):
        attend_tile(q, [(prompt, (b + j) * BLK, seen, masks) for j in range(2)], acc, tot)


def attend_far_kernel(pattern, q, w1, w2, w3, acc_in, tot_in, ours, theirs, acc, tot):
    acc[...] = acc_in[...]
    tot[...] = tot_in[...]
    core, order = plane_order()

    def window(source, ref):
        return window_block(pattern, order, core, source, 3, ref, 0)

    attend_tile(q, [window(1, w1), window(2, w2)], acc, tot)
    attend_tile(q, [window(3, w3)], acc, tot)
    for head in range(2):
        for i in range(PLANES):
            lo = head * SHARD + i * BLK
            total = jnp.sum(tot[lo : lo + BLK], axis=1, keepdims=True)
            part = (acc[lo : lo + BLK] / total).astype(jnp.bfloat16)
            lanes = slice(head * HD, (head + 1) * HD)
            ours[i * SLOTS : (i + 1) * SLOTS, lanes] = part[:SLOTS]
            j = OTHER[i]
            theirs[j * SLOTS : (j + 1) * SLOTS, lanes] = part[SLOTS:]


def attend(pattern, *args):
    return pl.pallas_call(
        attend_kernel,
        in_specs=[SMEM] + [VMEM] * len(args),
        out_specs=[VMEM] * 2,
        out_shape=[jax.ShapeDtypeStruct((2 * SHARD, HD), jnp.float32)] * 2,
        compiler_params=pltpu.CompilerParams(vmem_limit_bytes=VMEM_BYTES),
        name="attend",
    )(pattern, *args)


def attend_far(pattern, *args):
    return pl.pallas_call(
        attend_far_kernel,
        in_specs=[SMEM] + [VMEM] * len(args),
        out_specs=[VMEM] * 2,
        out_shape=[jax.ShapeDtypeStruct((PLANES * SLOTS, 2 * HD), jnp.bfloat16)] * 2,
        scratch_shapes=[pltpu.VMEM((2 * SHARD, HD), jnp.float32)] * 2,
        compiler_params=pltpu.CompilerParams(vmem_limit_bytes=VMEM_BYTES),
        name="attend_far",
    )(pattern, *args)


def out_kernel(chunks, ours, theirs, w0, w1, first, second, buf, sems):
    tile = D // TILES

    def copies(n):
        cols = pl.ds(n * tile, tile)
        return [
            pltpu.make_async_copy(w.at[:, cols], buf.at[n, pl.ds(i * 2 * HD, 2 * HD)], sems.at[n, i])
            for i, w in enumerate((w0, w1))
        ]

    for n in range(TILES):
        for copy in copies(n):
            copy.start()
    rows = jnp.concatenate(
        [
            jnp.concatenate([r[c * SLOTS : (c + 1) * SLOTS] for r in (ours, theirs)], axis=1)
            for c in chunks
        ],
        axis=0,
    )
    for n in range(TILES):
        for copy in copies(n):
            copy.wait()
        total = jnp.dot(rows, buf[n], preferred_element_type=jnp.float32)
        cols = slice(n * tile, (n + 1) * tile)
        first[:, cols] = total[:SLOTS].astype(first.dtype)
        second[:, cols] = total[SLOTS:].astype(second.dtype)


def project_out(chunks, dtype, ours, theirs, w_own, w_sib):
    hbm = pl.BlockSpec(memory_space=pltpu.HBM)
    return pl.pallas_call(
        functools.partial(out_kernel, chunks),
        in_specs=[VMEM] * 2 + [hbm] * 2,
        out_specs=[VMEM] * 2,
        out_shape=[jax.ShapeDtypeStruct((SLOTS, D), dtype)] * 2,
        scratch_shapes=[
            pltpu.VMEM((TILES, 4 * HD, D // TILES), jnp.bfloat16),
            pltpu.SemaphoreType.DMA((TILES, 2)),
        ],
        compiler_params=pltpu.CompilerParams(vmem_limit_bytes=VMEM_BYTES),
        name="project_out",
    )(ours, theirs, *[pltpu.with_memory_space_constraint(w, pltpu.HBM) for w in (w_own, w_sib)])


def body(
    rollout_rows, pack_dest, lengths, pattern, norm_gain, w_query, w_key, w_value, w_out, post_gain
):
    bf16 = jnp.bfloat16
    n_dp = lax.axis_size("dp")
    d = lax.axis_index("dp")
    per_peer = SLOTS // n_dp
    order_ids = jnp.arange(SLOTS, dtype=jnp.int32)

    target_dev = pack_dest // SHARD
    target_slot = pack_dest % SLOTS
    before = (target_dev[:, None] == target_dev[None, :]) & (order_ids[None, :] < order_ids[:, None])
    send_pos = target_dev * per_peer + jnp.sum(before.astype(jnp.int32), axis=1)
    placer = order_ids[:, None] == send_pos[None, :]
    send_rows = jnp.dot(placer.astype(bf16), rollout_rows, preferred_element_type=jnp.float32).astype(bf16)
    send_slots = jnp.sum(jnp.where(placer, target_slot[None, :], 0), axis=1)
    send = jnp.concatenate(
        [send_rows, jnp.broadcast_to(send_slots.astype(bf16)[:, None], (SLOTS, HD))], axis=1
    )
    width = D + HD
    got = lax.all_to_all(send.reshape(n_dp, per_peer, width), "dp", 0, 0, tiled=True)

    core, order = plane_order()
    first = send[:per_peer]
    piece = jnp.pad(first, ((0, 8 - per_peer), (0, 0)))
    column = [to(piece, OUT), to(piece, BACK), to(piece, FAR)]

    got = got.reshape(SLOTS, width)
    arrange = order_ids[:, None] == got[:, D].astype(jnp.int32)[None, :]
    packed = jnp.dot(arrange.astype(bf16), got[:, :D], preferred_element_type=jnp.float32).astype(bf16)
    packed = lax.optimization_barrier(packed)
    normed = rms_scale(packed.astype(jnp.float32), norm_gain).astype(bf16)

    near_o = to(normed, OUT)
    near_b = to(normed, BACK)
    own_s = to(normed, SIB)

    column, later, _ = lax.optimization_barrier((column, lengths, normed))
    cos_a, sin_a, cos_c, sin_c = tables(later)
    w_sib = to(w_out, SIB)
    early = jnp.concatenate([first] + [c[:per_peer] for c in column], axis=0)
    early_kv = early_keys(lengths, early, to(early, SIB), norm_gain, w_key, w_value, n_dp)
    near_o, near_b, early_kv, w_sib, cos_a = lax.optimization_barrier(
        (near_o, near_b, early_kv, w_sib, cos_a)
    )
    far_own = to(near_o, OUT)
    near_os = to(near_b, SIB)
    near_bs = to(near_o, SIB)
    q_a, kv_a = project_near(
        normed, own_s, near_o, near_os, near_b, near_bs, w_query, w_key, w_value, cos_a, sin_a
    )
    shifts = [[(s, s + k) for s in range(n_dp - k)] for k in (1, 2, 3)]
    kvs_a = [kv_a] + [lax.ppermute(kv_a, "dp", shift) for shift in shifts]
    early_kv, kv_a = lax.optimization_barrier((early_kv, kv_a))
    prompt = lax.all_to_all(early_kv, "dp", 0, 0, tiled=True)
    prompt = prompt.reshape(SHARD, 2 * HD)
    far_own, prompt = lax.optimization_barrier((far_own, prompt))
    far_s = to(far_own, SIB)
    q, kv_c = project_far(far_own, far_s, w_query, w_key, w_value, cos_c, sin_c, q_a)
    kvs_c = [lax.ppermute(kv_c, "dp", shift) for shift in shifts]
    acc, tot = attend(pattern, q, kv_a, kv_c, *kvs_a[1:], prompt)
    ours, theirs = attend_far(pattern, q, *kvs_c, acc, tot)

    theirs = to(theirs, SIB)
    sum_far, sum_o = project_out((3, 1), bf16, ours, theirs, w_out, w_sib)
    theirs, sum_far = lax.optimization_barrier((theirs, sum_far))
    own, sum_b = project_out((0, 2), jnp.float32, ours, theirs, w_out, w_sib)
    from_far = to(sum_far, OUT)
    from_b = to(sum_o, BACK)
    from_o = to((sum_b + from_far.astype(jnp.float32)).astype(bf16), OUT)
    summed = own + from_b.astype(jnp.float32) + from_o.astype(jnp.float32)
    result = packed.astype(jnp.float32) + rms_scale(summed, post_gain)
    return result.astype(bf16)


def solution(mesh):
    placed = (
        P(("dp", "tensor"), None),
        P(("dp", "tensor")),
        P(),
        P("dp", None),
        P(),
        P(None, "tensor"),
        P(None, "tensor"),
        P(None, "tensor"),
        P("tensor", None),
        P(),
    )
    return jax.shard_map(
        body, mesh=mesh, in_specs=placed, out_specs=P(("dp", "tensor"), None), check_vma=False
    )
```
